32 devices in a mesh: dp: 8 (over z, y), expert: 4 (over x, core).
Axes of the slice: x: 2, y: 2, z: 4, core: 2. Of those that a mesh axis runs over, the one named last changes fastest.
Arguments:
- patches: float32 [32, 512, 384], P(('dp', 'expert')), may hold values from -6 to 6
- image_ids: int32 [32, 512], P(('dp', 'expert')), may hold values from 0 to 5, never falling along the last dimension, each value on 1 to 196 neighbouring positions
- pad_mask: int32 [32, 512], P(('dp', 'expert')), may hold values 0 or 1
- ln1_gain: float32 [384], replicated, may hold values from 0.5 to 1.5
- ln1_bias: float32 [384], replicated, may hold values from -3 to 3
- w_qkv: float32 [384, 1152], replicated, may hold values from -0.3125 to 0.3125
- bias_qv: float32 [2, 384], replicated, may hold values from -3 to 3
- w_out: float32 [384, 384], replicated, may hold values from -1.25 to 1.25
- bias_out: float32 [384], replicated, may hold values from -3 to 3
- ln2_gain: float32 [384], replicated, may hold values from 0.5 to 1.5
- ln2_bias: float32 [384], replicated, may hold values from -2 to 2
- slot_keys: float32 [384, 8], replicated, may hold values from -0.625 to 0.625
- w_in: float32 [8, 384, 1536], P('expert'), may hold values from -1.25 to 1.25
- bias_in: float32 [8, 1536], P('expert'), may hold values from -3 to 3
- w_down: float32 [8, 1536, 384], P('expert'), may hold values from -0.3125 to 0.3125
- bias_down: float32 [8, 384], P('expert'), may hold values from -3 to 3
- cotangent: float32 [32, 512, 384], P(('dp', 'expert')), may hold values from -6 to 6
Outputs:
- activations: float32 [32, 512, 384], P(('dp', 'expert'))
- grad_patches: float32 [32, 512, 384], P(('dp', 'expert'))
- grad_ln1_gain: float32 [384], replicated
- grad_ln1_bias: float32 [384], replicated
- grad_w_qkv: float32 [384, 1152], replicated
- grad_bias_qv: float32 [2, 384], replicated
- grad_w_out: float32 [384, 384], replicated
- grad_bias_out: float32 [384], replicated
- grad_ln2_gain: float32 [384], replicated
- grad_ln2_bias: float32 [384], replicated
- grad_slot_keys: float32 [384, 8], replicated
- grad_w_in: float32 [8, 384, 1536], P('expert')
- grad_bias_in: float32 [8, 1536], P('expert')
- grad_w_down: float32 [8, 1536, 384], P('expert')
- grad_bias_down: float32 [8, 384], P('expert')
The draws below stay inside these ranges and needn't reach their ends.
All inputs are finite; a program needn't handle non-finite values. No bound on the sum of `pad_mask` on one device may be relied on, other than what follows from the above.
Results may differ from the reference program's by a relative error of at most 0.0003.
Values sent between devices are 32-bit elements; how exact they have to be, the bound alone decides.
A program may use at most 128 MiB of HBM per device.

```python
import math
import jax
import jax.numpy as jnp
import numpy as np
from jax import lax

D = 384
HEADS = 6
HEAD_DIM = 64
FF = 1536
EXPERTS = 8
SEQ = 512
BLOCK = 512
IMG = 196
ROWS = 32


def with_ends(drawn, stream_key, least, high):
    longest = drawn.shape.index(max(drawn.shape))
    spots = []
    for shift in (0, 1):
        where = [jax.random.randint(jax.random.fold_in(stream_key, axis), (), 0, length) for axis, length in enumerate(drawn.shape)]
        where[longest] = (where[longest] + shift) % drawn.shape[longest]
        spots.append(tuple(where))
    return drawn.at[spots[0]].set(least).at[spots[1]].set(high)


def block_levels(key, shape, shards, low, high):
    level, own = 1.0, jax.random.fold_in(key, 6)
    for position, parts in shards:
        draws = jnp.exp(jax.random.uniform(jax.random.fold_in(own, position), (parts,), jnp.float32, low / len(shards), high / len(shards)))
        level = level * jnp.repeat(draws, shape[position] // parts).reshape([-1 if axis == position else 1 for axis in range(len(shape))])
    return level


def split_up(number_of, total, limit, lean):
    weights = [(1 << 20) // math.isqrt(grade ** lean) + 1 for grade in range(2, number_of + 1)]
    rest, holding = total - limit - (number_of - 1), [1] * (number_of - 1)
    while rest > 0:
        free = [i for i in range(number_of - 1) if holding[i] < limit]
        pool, left = sum([weights[i] for i in free]), rest
        for i in free:
            extra = min(limit - holding[i], max(1, left * weights[i] // pool), rest)
            holding[i] = holding[i] + extra
            rest = rest - extra
    return np.array([limit] + holding)


def uneven(own_key, count, total, most, skew):
    if count == 2:
        one = jax.random.randint(own_key, (), max(1, total - most), min(most, total - 1) + 1)
        return jnp.stack([one, total - one])
    tallies = jnp.asarray(split_up(count, total, most, skew), jnp.int32)
    couples = (count - 1) // 2
    donor, receiver = tallies[1:1 + 2 * couples:2], tallies[2:2 + 2 * couples:2]
    room = jnp.minimum(donor - 1, most - receiver)
    passed = jax.random.randint(jax.random.fold_in(own_key, 1), (couples,), 0, 1 << 20) % (room + 1)
    tallies = tallies.at[1:1 + 2 * couples:2].set(donor - passed).at[2:2 + 2 * couples:2].set(receiver + passed)
    return tallies[jax.random.permutation(jax.random.fold_in(own_key, 2), count)]


def noise(rng, extent, deviation, limit, split=(), dtype=jnp.bfloat16):
    factor_of = block_levels(rng, extent, split, -0.22, 0.18) if split else 1.0
    entries = jax.random.normal(rng, extent, jnp.float32) * deviation * factor_of
    return jnp.minimum(jnp.maximum(entries, -limit), limit).astype(dtype)


def setup_inputs(seed: int = 0) -> dict:
    keys = jax.random.split(jax.random.key(seed), 18)
    patches = noise(keys[0], (ROWS, SEQ, D), 1.0, 6.0, ((0, 32),), jnp.float32)
    image_ids = jax.vmap(lambda own: jnp.searchsorted(jnp.cumsum(uneven(own, 2 * SEQ // IMG + 1, SEQ, IMG, 0)), jnp.arange(SEQ), side="right"))(jax.random.split(keys[1], ROWS)).reshape((ROWS, SEQ)).astype(jnp.int32)
    pad_mask = with_ends((jax.random.randint(keys[2], (ROWS, SEQ), 0, 8) < 7).astype(jnp.int32), jax.random.fold_in(keys[2], 1), 0, 1)
    ln1_gain = jnp.clip(1.0 + 0.1 * jax.random.normal(keys[3], (D,), jnp.float32), 0.5, 1.5)
    ln1_bias = noise(keys[4], (D,), 0.3, 3.0, (), jnp.float32)
    w_qkv = noise(keys[5], (D, 3 * D), D ** -0.5, 0.3125, (), jnp.float32)
    bias_qv = noise(keys[6], (2, D), 0.3, 3.0, (), jnp.float32)
    w_out = noise(keys[7], (D, D), (D // 16) ** -0.5, 1.25, (), jnp.float32)
    bias_out = noise(keys[8], (D,), 0.3, 3.0, (), jnp.float32)
    ln2_gain = jnp.clip(1.0 + 0.1 * jax.random.normal(keys[9], (D,), jnp.float32), 0.5, 1.5)
    ln2_bias = noise(keys[10], (D,), 0.2, 2.0, (), jnp.float32)
    slot_keys = noise(keys[11], (D, EXPERTS), (D // 4) ** -0.5, 0.625, (), jnp.float32)
    w_in = noise(keys[12], (EXPERTS, D, FF), (D // 16) ** -0.5, 1.25, ((0, 4),), jnp.float32)
    bias_in = noise(keys[13], (EXPERTS, FF), 0.5, 3.0, ((0, 4),), jnp.float32)
    w_down = noise(keys[14], (EXPERTS, FF, D), (FF // 4) ** -0.5, 0.3125, ((0, 4),), jnp.float32)
    bias_down = noise(keys[15], (EXPERTS, D), 0.5, 3.0, ((0, 4),), jnp.float32)
    cotangent = noise(keys[16], (ROWS, SEQ, D), 1.0, 6.0, ((0, 32),), jnp.float32)
    return dict(patches=patches, image_ids=image_ids, pad_mask=pad_mask, ln1_gain=ln1_gain, ln1_bias=ln1_bias, w_qkv=w_qkv, bias_qv=bias_qv, w_out=w_out, bias_out=bias_out, ln2_gain=ln2_gain, ln2_bias=ln2_bias, slot_keys=slot_keys, w_in=w_in, bias_in=bias_in, w_down=w_down, bias_down=bias_down, cotangent=cotangent)


EPSILON = 1e-06
NEGATIVE = -1e+30
PRECISE = lax.Precision.HIGHEST

@jax.custom_vjp
def low(v):
    return lax.optimization_barrier(v.astype(jnp.bfloat16)).astype(jnp.float32)

@jax.custom_vjp
def low_back(v):
    return v

def low_keep(v):
    return (low(v), None)

def low_pass(kept, grad):
    return (grad,)

def back_keep(v):
    return (v, None)

def back_low(kept, grad):
    return (low(grad),)
low.defvjp(low_keep, low_pass)
low_back.defvjp(back_keep, back_low)

def product(left, right):
    return jnp.dot(left, right, precision=PRECISE)

def layer_norm(values, gain, shift):
    center = values - lax.optimization_barrier(jnp.mean(values, -1, keepdims=True))
    spread = lax.optimization_barrier(jnp.mean(center * center, -1, keepdims=True))
    return center * lax.rsqrt(spread + EPSILON) * gain + shift

def gelu_exact(values):
    return 0.5 * values * (1.0 + jax.scipy.special.erf(values / math.sqrt(2.0)))

def softmax_along(values, axis):
    peak = lax.optimization_barrier(jnp.max(values, axis, keepdims=True))
    expo = jnp.exp(values - peak)
    return expo / lax.optimization_barrier(jnp.sum(expo, axis, keepdims=True))

def attend_block(queries, query_ids, keys_all, values_all, key_ids):
    scores = jnp.einsum('qhd,khd->hqk', queries, keys_all, precision=PRECISE) / math.sqrt(HEAD_DIM)
    same = query_ids[:, None] == key_ids[None, :]
    weights = softmax_along(jnp.where(same[None], scores, NEGATIVE), -1)
    return jnp.einsum('hqk,khd->qhd', weights, values_all, precision=PRECISE)

def attention_row(row, row_ids, ln1_gain, ln1_bias, w_qkv, bias_qv, w_out, bias_out):
    length = row.shape[0]
    width = row.shape[1]
    normed = layer_norm(row, ln1_gain, ln1_bias)
    shift = jnp.concatenate([bias_qv[0], jnp.zeros_like(bias_qv[0]), bias_qv[1]])
    joined = product(normed, w_qkv) + shift
    queries = joined[:, :width].reshape(length, HEADS, HEAD_DIM)
    keys_all = joined[:, width:2 * width].reshape(length, HEADS, HEAD_DIM)
    values_all = joined[:, 2 * width:].reshape(length, HEADS, HEAD_DIM)
    count = length // BLOCK

    def one_block(pair):
        return attend_block(pair[0], pair[1], keys_all, values_all, row_ids)
    context = lax.map(jax.checkpoint(one_block), (queries.reshape(count, BLOCK, HEADS, HEAD_DIM), row_ids.reshape(count, BLOCK)))
    return row + product(context.reshape(length, width), w_out) + bias_out

def experts_apply(slots, w_in, bias_in, w_down, bias_down):
    inner = jnp.einsum('ed,edf->ef', slots, w_in, precision=PRECISE) + bias_in
    return jnp.einsum('ef,efd->ed', gelu_exact(inner), w_down, precision=PRECISE) + bias_down

def forward(patches, ln1_gain, ln1_bias, w_qkv, bias_qv, w_out, bias_out, ln2_gain, ln2_bias, slot_keys, w_in, bias_in, w_down, bias_down, image_ids, pad_mask):

    def one_row(pair):
        return attention_row(pair[0], pair[1], ln1_gain, ln1_bias, w_qkv, bias_qv, w_out, bias_out)
    resid = lax.map(jax.checkpoint(one_row), (patches, image_ids))
    flat = resid.reshape(-1, resid.shape[-1])
    normed = layer_norm(flat, ln2_gain, ln2_bias)
    logits = product(normed, slot_keys)
    live = pad_mask.reshape(-1, 1) > 0
    dispatch = softmax_along(jnp.where(live, logits, NEGATIVE), 0)
    slots = product(dispatch.T, normed)
    slot_out = experts_apply(slots, w_in, bias_in, w_down, bias_down)
    combine = softmax_along(logits, -1)
    return (flat + product(combine, slot_out)).reshape(patches.shape)

def reference(patches, image_ids, pad_mask, ln1_gain, ln1_bias, w_qkv, bias_qv, w_out, bias_out, ln2_gain, ln2_bias, slot_keys, w_in, bias_in, w_down, bias_down, cotangent):

    def wrapped(*floats):
        return forward(*floats, image_ids, pad_mask)
    result, back = jax.vjp(wrapped, patches, ln1_gain, ln1_bias, w_qkv, bias_qv, w_out, bias_out, ln2_gain, ln2_bias, slot_keys, w_in, bias_in, w_down, bias_down)
    grads = back(cotangent)
    return (result, grads[0], grads[1], grads[2], grads[3], grads[4], grads[5], grads[6], grads[7], grads[8], grads[9], grads[10], grads[11], grads[12], grads[13])
```

```python
import functools
import math

import jax
import jax.numpy as jnp
from jax import lax
from jax.experimental import pallas as pl
from jax.experimental.pallas import tpu as pltpu
from jax.sharding import PartitionSpec as P

HEADS = 6
HEAD_DIM = 64
LANES = 128
EPSILON = 1e-06
NEGATIVE = -1e30
HIGH = lax.Precision.HIGH
BF = jnp.bfloat16
F32 = jnp.float32
MESH = pl.DeviceIdType.MESH
VMEM = pl.BlockSpec(memory_space=pltpu.VMEM)
ANY = pl.BlockSpec(memory_space=pl.ANY)


def dot(left, right, dim_left, dim_right, precision=HIGH):
    return lax.dot_general(
        left, right, (((dim_left,), (dim_right,)), ((), ())), precision=precision, preferred_element_type=F32
    )


def parts(value):
    high = value.astype(BF)
    return high, (value - high.astype(F32)).astype(BF)


def norm_stats(values):
    center = values - jnp.mean(values, -1, keepdims=True)
    spread = jnp.mean(center * center, -1, keepdims=True)
    scale = lax.rsqrt(spread + EPSILON)
    return center * scale, scale


def column(row):
    return jnp.broadcast_to(row, (8, row.shape[1])).T[:, :1]


def to_tiles(rows):
    return jnp.stack([jnp.concatenate([rows[e : e + 1, LANES * i : LANES * (i + 1)] for i in range(8)], 0) for e in range(rows.shape[0])], 0)


def from_tiles(tiles, first, count):
    return jnp.concatenate([tiles[:, first + i, :] for i in range(count)], -1)


def front_kernel(x_ref, ids_ref, live_ref, g1_ref, b1_ref, wqkv_ref, bqv_ref, wout_ref, bout_ref, g2_ref, b2_ref,
                 keys_ref, cot_ref, resid_ref, joined_ref, context_ref, attn_ref, logits_ref, stats_ref, block_ref):
    x = x_ref[0]
    length, width = x.shape
    hat, _ = norm_stats(x)
    normed = hat * g1_ref[...] + b1_ref[...]
    joined = dot(wqkv_ref[...], normed, 0, 1)
    bias = jnp.broadcast_to(bqv_ref[0:1], (8, width)).T[:, :1]
    bias_v = jnp.broadcast_to(bqv_ref[1:2], (8, width)).T[:, :1]
    scale = 1.0 / math.sqrt(HEAD_DIM)
    joined_ref[0:width] = (joined[:width] + bias) * scale
    joined_ref[width : 2 * width] = joined[width : 2 * width]
    joined_ref[2 * width :] = joined[2 * width :] + bias_v
    ids = ids_ref[...].astype(F32)
    block_ref[...] = jnp.where(column(ids) == ids, 0.0, NEGATIVE)
    half = length // 2
    for h in range(HEADS):
        at = HEAD_DIM * h
        q_hi, q_lo = parts(joined_ref[at : at + HEAD_DIM])
        k_hi, k_lo = parts(joined_ref[width + at : width + at + HEAD_DIM])
        v_hi, v_lo = parts(joined_ref[2 * width + at : 2 * width + at + HEAD_DIM])
        queries = jnp.concatenate([q_hi, q_hi, q_lo], 0)
        keys = jnp.concatenate([k_hi, k_lo, k_hi], 0).T
        values = jnp.concatenate([v_hi, v_lo], 0)
        for b in range(2):
            span = slice(half * b, half * (b + 1))
            scores = dot(keys, queries[:, span], 1, 0, None) + block_ref[:, span]
            expo = jnp.exp(scores - jnp.max(scores, 0, keepdims=True))
            attn = expo * (1.0 / jnp.sum(expo, 0, keepdims=True))
            attn_ref[h, :, span] = attn
            p_hi, p_lo = parts(attn)
            both = dot(values, p_hi, 1, 0, None)
            context_ref[at : at + HEAD_DIM, span] = both[:HEAD_DIM] + both[HEAD_DIM:] + dot(v_hi, p_lo, 1, 0, None)
    resid = x + dot(context_ref[...], wout_ref[...], 0, 0) + bout_ref[...]
    resid_ref[...] = resid
    hat2, _ = norm_stats(resid)
    normed2 = hat2 * g2_ref[...] + b2_ref[...]
    logits = dot(keys_ref[...], normed2, 0, 1)
    logits_ref[...] = logits
    masked = jnp.where(live_ref[...] > 0, logits, NEGATIVE)
    peak = jnp.max(masked, 1, keepdims=True)
    expo = jnp.exp(masked - peak)
    total = jnp.sum(expo, 1, keepdims=True)
    summed = dot(expo, normed2, 1, 0)
    top = jnp.max(logits, 0, keepdims=True)
    comb = jnp.exp(logits - top)
    comb = comb * (1.0 / jnp.sum(comb, 0, keepdims=True))
    part_out = dot(comb, cot_ref[0], 1, 0)
    experts = logits.shape[0]
    rows = jnp.concatenate([summed, part_out, jnp.broadcast_to(peak, (experts, LANES)), jnp.broadcast_to(total, (experts, LANES))], 1)
    stats_ref[...] = to_tiles(rows)


def merge(tiles):
    peaks = [tile[:, 6:7, :] for tile in tiles]
    peak = functools.reduce(jnp.maximum, peaks)
    row = lax.broadcasted_iota(jnp.int32, tiles[0].shape, 1)
    weighted = (row < 3) | (row == 7)
    total = None
    for tile, own in zip(tiles, peaks):
        scaled = jnp.where(weighted, tile * jnp.exp(own - peak), tile)
        total = scaled if total is None else total + scaled
    return jnp.where(row == 6, peak, total)


def gelu_parts(inner):
    phi = 0.5 * (1.0 + lax.erf(inner * (1.0 / math.sqrt(2.0))))
    density = jnp.exp(-0.5 * inner * inner) * (1.0 / math.sqrt(2.0 * math.pi))
    return inner * phi, phi + inner * density


def rows_to_columns(rows):
    pad = -rows.shape[0] % 8
    if pad:
        rows = jnp.concatenate([rows, jnp.zeros((pad, LANES), F32)], 0)
    return rows.T


def times_columns(cols, count, w_ref, e, lanes):
    wide = [jnp.broadcast_to(cols[:, i : i + 1], (LANES, LANES)) for i in range(count)]
    rows = []
    for j in range(lanes):
        acc = None
        for i in range(count):
            term = wide[i] * w_ref[e, LANES * i : LANES * (i + 1), LANES * j : LANES * (j + 1)]
            term = jnp.sum(term.reshape(LANES // 8, 8, LANES), 0)
            acc = term if acc is None else acc + term
        rows.append(jnp.sum(acc, 0, keepdims=True))
    return jnp.concatenate(rows, 0)


def times_rows(rows, count, w_ref, e, blocks):
    out = []
    for i in range(blocks):
        acc = None
        for j in range(count):
            term = rows[j : j + 1] * w_ref[e, LANES * i : LANES * (i + 1), LANES * j : LANES * (j + 1)]
            acc = term if acc is None else acc + term
        out.append(jnp.sum(acc.T, 0, keepdims=True))
    return jnp.concatenate(out, 0)


def expert_kernel(n_dp, n_ex, stats_ref, win_hbm, bin_ref, wdown_hbm, bdown_ref, shared_ref, own_ref, inner_ref,
                  win, wdown, near, mine, far, send_near, recv_near, send_far, recv_far, send_out, recv_out, got, loads):
    dp, ex = lax.axis_index("dp"), lax.axis_index("expert")
    owned = win.shape[0]
    barrier = pltpu.get_barrier_semaphore()
    for i in range(1, n_ex):
        pl.semaphore_signal(barrier, inc=1, device_id=(dp, lax.rem(ex + i, n_ex)), device_id_type=MESH)
    for i in range(1, n_dp):
        pl.semaphore_signal(barrier, inc=1, device_id=(lax.rem(dp + i, n_dp), ex), device_id_type=MESH)
    load_in = pltpu.make_async_copy(win_hbm, win, loads.at[0])
    load_in.start()
    load_down = pltpu.make_async_copy(wdown_hbm, wdown, loads.at[1])
    load_down.start()
    pl.semaphore_wait(barrier, n_ex + n_dp - 2)
    copies = []
    for i in range(1, n_ex):
        to = lax.rem(ex + i, n_ex)
        copy = pltpu.make_async_remote_copy(
            src_ref=stats_ref.at[pl.ds(to * owned, owned)], dst_ref=near.at[i - 1], send_sem=send_near.at[i - 1],
            recv_sem=recv_near.at[i - 1], device_id=(dp, to), device_id_type=MESH)
        copy.start()
        copies.append(copy)
    for copy in copies:
        copy.wait()
    mine[...] = merge([stats_ref[pl.ds(ex * owned, owned)]] + [near[i] for i in range(n_ex - 1)])
    copies = []
    for i in range(1, n_dp):
        to = lax.rem(dp + i, n_dp)
        copy = pltpu.make_async_remote_copy(
            src_ref=mine, dst_ref=far.at[i - 1], send_sem=send_far.at[i - 1], recv_sem=recv_far.at[i - 1],
            device_id=(to, ex), device_id_type=MESH)
        copy.start()
        copies.append(copy)
    for copy in copies:
        copy.wait()
    tiles = merge([mine[...]] + [far[i] for i in range(n_dp - 1)])
    load_in.wait()
    load_down.wait()
    blocks, wide = win.shape[1] // LANES, win.shape[2] // LANES
    for e in range(owned):
        tile = tiles[e]
        slots = tile[0:blocks] / tile[7:8]
        d_out = tile[3 : 3 + blocks]
        bias = jnp.concatenate([bin_ref[e : e + 1, LANES * j : LANES * (j + 1)] for j in range(wide)], 0)
        inner = times_columns(rows_to_columns(slots), blocks, win, e, wide) + bias
        hidden, slope = gelu_parts(inner)
        bias = jnp.concatenate([bdown_ref[e : e + 1, LANES * j : LANES * (j + 1)] for j in range(blocks)], 0)
        out = times_columns(rows_to_columns(hidden), wide, wdown, e, blocks) + bias
        d_inner = times_rows(d_out, blocks, wdown, e, wide) * slope
        d_slots = times_rows(d_inner, wide, win, e, blocks)
        along = jnp.sum(slots * d_slots, keepdims=True)
        lane = lax.broadcasted_iota(jnp.int32, (1, LANES), 1)
        last = jnp.where(lane < LANES // 2, tile[7:8], along)
        shared_ref[ex * owned + e] = jnp.concatenate([out, d_slots, tile[6:7], last], 0)
        own_ref[e] = jnp.concatenate([slots, d_out, jnp.zeros((2, LANES), F32)], 0)
        got[e] = jnp.concatenate([out, d_slots, tile[6:7], last], 0)
        inner_ref[e] = jnp.concatenate([hidden, d_inner], 0)
    copies = []
    for i in range(1, n_ex):
        to = lax.rem(ex + i, n_ex)
        copy = pltpu.make_async_remote_copy(
            src_ref=got, dst_ref=shared_ref.at[pl.ds(ex * owned, owned)], send_sem=send_out.at[i - 1],
            recv_sem=recv_out.at[i - 1], device_id=(dp, to), device_id_type=MESH)
        copy.start()
        copies.append(copy)
    for copy in copies:
        copy.wait()


def norm_back(grad, hat, scale, gain):
    g = grad * gain
    return scale * (g - jnp.mean(g, -1, keepdims=True) - hat * jnp.mean(g * hat, -1, keepdims=True))


def back_kernel(x_ref, live_ref, g1_ref, b1_ref, wqkv_ref, wout_ref, g2_ref, b2_ref, keys_ref, cot_ref, resid_ref,
                joined_ref, context_ref, attn_ref, logits_ref, shared_ref, own_ref, inner_ref,
                act_ref, gx_ref, gwqkv_ref, gwout_ref, small_ref, gwin_hbm, gwdown_hbm, gin, gdown, djoined_ref, sems):
    length, width = resid_ref.shape
    owned = own_ref.shape[0]
    blocks = width // LANES
    wide = gin.shape[2] // LANES
    writes = []
    for e in range(owned):
        slot_cols = rows_to_columns(own_ref[e])
        hidden_cols = rows_to_columns(inner_ref[e])
        for i in range(blocks):
            col = jnp.broadcast_to(slot_cols[:, i : i + 1], (LANES, LANES))
            for j in range(wide):
                gin[e, LANES * i : LANES * (i + 1), LANES * j : LANES * (j + 1)] = col * inner_ref[e, wide + j : wide + j + 1]
        copy = pltpu.make_async_copy(gin.at[e], gwin_hbm.at[e], sems.at[2 * e])
        copy.start()
        writes.append(copy)
        for j in range(wide):
            col = jnp.broadcast_to(hidden_cols[:, j : j + 1], (LANES, LANES))
            for i in range(blocks):
                gdown[e, LANES * j : LANES * (j + 1), LANES * i : LANES * (i + 1)] = col * own_ref[e, 3 + i : 4 + i]
        copy = pltpu.make_async_copy(gdown.at[e], gwdown_hbm.at[e], sems.at[2 * e + 1])
        copy.start()
        writes.append(copy)
    shared = shared_ref[...]
    slot_out = from_tiles(shared, 0, 3)
    d_slots = from_tiles(shared, 3, 3)
    peak = shared[:, 6, 0:1]
    total = shared[:, 7, 0:1]
    along = shared[:, 7, LANES - 1 : LANES]
    cot = cot_ref[0]
    resid = resid_ref[...]
    hat2, scale2 = norm_stats(resid)
    normed2 = hat2 * g2_ref[...] + b2_ref[...]
    logits = logits_ref[...]
    dispatch = jnp.exp(jnp.where(live_ref[...] > 0, logits, NEGATIVE) - peak) / total
    comb = jnp.exp(logits - jnp.max(logits, 0, keepdims=True))
    comb = comb * (1.0 / jnp.sum(comb, 0, keepdims=True))
    act_ref[0] = resid + dot(comb, slot_out, 0, 0)
    d_comb = dot(slot_out, cot, 1, 1)
    d_logits = comb * (d_comb - jnp.sum(comb * d_comb, 0, keepdims=True))
    d_logits = d_logits + dispatch * (dot(d_slots, normed2, 1, 1) - along)
    d_normed2 = dot(jnp.concatenate([dispatch, d_logits], 0), jnp.concatenate([d_slots, keys_ref[...].T], 0), 0, 0)
    small_ref[8:16] = dot(d_logits, normed2, 1, 0)
    small_ref[5:6] = jnp.sum(d_normed2 * hat2, 0, keepdims=True)
    small_ref[6:7] = jnp.sum(d_normed2, 0, keepdims=True)
    d_resid = cot + norm_back(d_normed2, hat2, scale2, g2_ref[...])
    context = context_ref[...]
    gwout_ref[...] = dot(context, d_resid, 1, 0)
    small_ref[4:5] = jnp.sum(d_resid, 0, keepdims=True)
    d_context = dot(wout_ref[...], d_resid, 1, 1)
    along_q = d_context * context
    scale = 1.0 / math.sqrt(HEAD_DIM)
    half = length // 2
    for h in range(HEADS):
        at = HEAD_DIM * h
        span = slice(at, at + HEAD_DIM)
        q_hi, q_lo = parts(joined_ref[at : at + HEAD_DIM])
        k_hi, k_lo = parts(joined_ref[width + at : width + at + HEAD_DIM])
        v_hi, v_lo = parts(joined_ref[2 * width + at : 2 * width + at + HEAD_DIM])
        o_hi, o_lo = parts(d_context[span])
        rowsum = jnp.sum(along_q[span], 0, keepdims=True)
        values = jnp.concatenate([v_hi, v_lo, v_hi], 0).T
        d_out = jnp.concatenate([o_hi, o_hi, o_lo], 0)
        keys = jnp.concatenate([k_hi, k_lo], 0)
        queries = jnp.concatenate([q_hi, q_lo], 0)
        outs = jnp.concatenate([o_hi, o_lo], 0)
        d_v = d_k = None
        for b in range(2):
            part = slice(half * b, half * (b + 1))
            attn = attn_ref[h, :, part]
            d_attn = dot(values, d_out[:, part], 1, 0, None)
            d_scores = attn * (d_attn - rowsum[:, part])
            p_hi, p_lo = parts(attn)
            s_hi, s_lo = parts(d_scores)
            both = dot(keys, s_hi, 1, 0, None)
            d_q = both[:HEAD_DIM] + both[HEAD_DIM:] + dot(k_hi, s_lo, 1, 0, None)
            djoined_ref[span, part] = d_q * scale
            both = dot(outs[:, part], p_hi, 1, 1, None)
            term = both[:HEAD_DIM] + both[HEAD_DIM:] + dot(o_hi[:, part], p_lo, 1, 1, None)
            d_v = term if d_v is None else d_v + term
            both = dot(queries[:, part], s_hi, 1, 1, None)
            term = both[:HEAD_DIM] + both[HEAD_DIM:] + dot(q_hi[:, part], s_lo, 1, 1, None)
            d_k = term if d_k is None else d_k + term
        djoined_ref[width + at : width + at + HEAD_DIM] = d_k
        djoined_ref[2 * width + at : 2 * width + at + HEAD_DIM] = d_v
    d_joined = djoined_ref[...]
    x = x_ref[0]
    hat, scale1 = norm_stats(x)
    normed = hat * g1_ref[...] + b1_ref[...]
    gwqkv_ref[...] = dot(normed, d_joined, 0, 1)
    sums = dot(jnp.ones((8, length), F32), d_joined, 1, 1)
    small_ref[2:3] = sums[0:1, :width]
    small_ref[3:4] = sums[0:1, 2 * width :]
    d_normed = dot(d_joined, wqkv_ref[...], 0, 1)
    small_ref[0:1] = jnp.sum(d_normed * hat, 0, keepdims=True)
    small_ref[1:2] = jnp.sum(d_normed, 0, keepdims=True)
    small_ref[7:8] = jnp.zeros((1, width), F32)
    gx_ref[0] = d_resid + norm_back(d_normed, hat, scale1, g1_ref[...])
    for copy in writes:
        copy.wait()


def sds(*shape):
    return jax.ShapeDtypeStruct(shape, F32)


def solution(mesh):
    n_dp, n_ex = mesh.shape["dp"], mesh.shape["expert"]

    def on_device(patches, image_ids, pad_mask, ln1_gain, ln1_bias, w_qkv, bias_qv, w_out, bias_out, ln2_gain, ln2_bias,
                  slot_keys, w_in, bias_in, w_down, bias_down, cotangent):
        _, length, width = patches.shape
        owned, _, hidden = w_in.shape
        experts = owned * n_ex
        row = lambda v: v.reshape(1, -1)
        g1, b1, bo, g2, b2 = map(row, (ln1_gain, ln1_bias, bias_out, ln2_gain, ln2_bias))
        resid, joined, context, attn, logits, stats = pl.pallas_call(
            front_kernel,
            out_shape=(sds(length, width), sds(3 * width, length), sds(width, length), sds(HEADS, length, length),
                       sds(experts, length), sds(experts, 8, LANES)),
            in_specs=[VMEM] * 13,
            out_specs=[VMEM] * 6,
            scratch_shapes=[pltpu.VMEM((length, length), F32)],
            compiler_params=pltpu.CompilerParams(vmem_limit_bytes=40 << 20),
            name="front",
        )(patches, image_ids, pad_mask, g1, b1, w_qkv, bias_qv, w_out, bo, g2, b2, slot_keys, cotangent)
        shared, own, inner = pl.pallas_call(
            functools.partial(expert_kernel, n_dp, n_ex),
            out_shape=(sds(experts, 8, LANES), sds(owned, 8, LANES), sds(owned, 2 * hidden // LANES, LANES)),
            in_specs=[VMEM, ANY, VMEM, ANY, VMEM],
            out_specs=[VMEM] * 3,
            scratch_shapes=[
                pltpu.VMEM(w_in.shape, F32), pltpu.VMEM(w_down.shape, F32),
                pltpu.VMEM((n_ex - 1, owned, 8, LANES), F32), pltpu.VMEM((owned, 8, LANES), F32),
                pltpu.VMEM((n_dp - 1, owned, 8, LANES), F32),
                pltpu.SemaphoreType.DMA((n_ex - 1,)), pltpu.SemaphoreType.DMA((n_ex - 1,)),
                pltpu.SemaphoreType.DMA((n_dp - 1,)), pltpu.SemaphoreType.DMA((n_dp - 1,)),
                pltpu.SemaphoreType.DMA((n_ex - 1,)), pltpu.SemaphoreType.DMA((n_ex - 1,)),
                pltpu.VMEM((owned, 8, LANES), F32), pltpu.SemaphoreType.DMA((2,)),
            ],
            compiler_params=pltpu.CompilerParams(collective_id=0, has_side_effects=True, vmem_limit_bytes=24 << 20),
            name="experts",
        )(stats, w_in, bias_in, w_down, bias_down)
        act, gx, gwqkv, gwout, small, gwin, gwdown = pl.pallas_call(
            back_kernel,
            out_shape=(sds(1, length, width), sds(1, length, width), sds(*w_qkv.shape), sds(*w_out.shape), sds(16, width),
                       sds(*w_in.shape), sds(*w_down.shape)),
            in_specs=[VMEM] * 18,
            out_specs=[VMEM] * 5 + [ANY] * 2,
            scratch_shapes=[pltpu.VMEM(w_in.shape, F32), pltpu.VMEM(w_down.shape, F32), pltpu.VMEM((3 * width, length), F32),
                            pltpu.SemaphoreType.DMA((2 * owned,))],
            compiler_params=pltpu.CompilerParams(vmem_limit_bytes=56 << 20),
            name="back",
        )(patches, pad_mask, g1, b1, w_qkv, w_out, g2, b2, slot_keys, cotangent, resid, joined, context, attn, logits,
          shared, own, inner)
        gwqkv, gwout, small = lax.psum((gwqkv, gwout, small), ("dp", "expert"))
        flat = lambda i: small[i].reshape(width)
        d_inner = inner[:, hidden // LANES :].reshape(owned, hidden)
        d_out = own[:, 3 : 3 + width // LANES].reshape(owned, width)
        return (act, gx, flat(0), flat(1), gwqkv, small[2:4], gwout, flat(4), flat(5), flat(6), small[8:16].T, gwin, d_inner,
                gwdown, d_out)

    rows = P(("dp", "expert"), None, None)
    flags = P(("dp", "expert"), None)
    e3, e2 = P("expert", None, None), P("expert", None)
    return jax.shard_map(
        on_device,
        mesh=mesh,
        in_specs=(rows, flags, flags) + (P(),) * 9 + (e3, e2, e3, e2, rows),
        out_specs=(rows, rows) + (P(),) * 9 + (e3, e2, e3, e2),
        check_vma=False,
    )
```

```python
import functools
import math

import jax
import jax.numpy as jnp
from jax import lax
from jax.experimental import pallas as pl
from jax.experimental.pallas import tpu as pltpu
from jax.sharding import PartitionSpec as P

HEADS = 6
HEAD_DIM = 64
LANES = 128
EPSILON = 1e-06
NEGATIVE = -1e30
HIGH = lax.Precision.HIGH
BF = jnp.bfloat16
F32 = jnp.float32
MESH = pl.DeviceIdType.MESH
FRONT_VMEM = ROUTE_VMEM = BACK_VMEM = 60 << 20
FINISH_VMEM = 8 << 20
VMEM = pl.BlockSpec(memory_space=pltpu.VMEM)
ANY = pl.BlockSpec(memory_space=pl.ANY)


def dot(left, right, dim_left, dim_right, precision=HIGH):
    return lax.dot_general(
        left, right, (((dim_left,), (dim_right,)), ((), ())), precision=precision, preferred_element_type=F32
    )


def parts(value):
    high = value.astype(BF)
    return high, (value - high.astype(F32)).astype(BF)


def norm_stats(values):
    center = values - jnp.mean(values, -1, keepdims=True)
    spread = jnp.mean(center * center, -1, keepdims=True)
    scale = lax.rsqrt(spread + EPSILON)
    return center * scale, scale


def column(row):
    return jnp.broadcast_to(row, (8, row.shape[1])).T[:, :1]


def load(sources, targets, sems):
    copies = [pltpu.make_async_copy(src, dst, sems.at[i]) for i, (src, dst) in enumerate(zip(sources, targets))]
    for copy in copies:
        copy.start()
    return copies


def greet(n_dp, n_ex, dp, ex):
    barrier = pltpu.get_barrier_semaphore()
    for i in range(1, n_ex):
        pl.semaphore_signal(barrier, inc=1, device_id=(dp, lax.rem(ex + i, n_ex)), device_id_type=MESH)
    for i in range(1, n_dp):
        pl.semaphore_signal(barrier, inc=1, device_id=(lax.rem(dp + i, n_dp), ex), device_id_type=MESH)
    return lambda: pl.semaphore_wait(barrier, n_ex + n_dp - 2)


def send(src, dst, out_sem, in_sem, dp, ex):
    copy = pltpu.make_async_remote_copy(
        src_ref=src, dst_ref=dst, send_sem=out_sem, recv_sem=in_sem, device_id=(dp, ex), device_id_type=MESH)
    copy.start()
    return copy


def as_row(ref):
    return ref[...].reshape(1, -1)


def to_tiles(rows):
    return jnp.stack([jnp.concatenate([rows[e : e + 1, LANES * i : LANES * (i + 1)] for i in range(8)], 0) for e in range(rows.shape[0])], 0)


def from_tiles(tiles, first, count):
    return jnp.concatenate([tiles[:, first + i, :] for i in range(count)], -1)


def merge(tiles):
    peaks = [tile[:, 6:7, :] for tile in tiles]
    peak = functools.reduce(jnp.maximum, peaks)
    row = lax.broadcasted_iota(jnp.int32, tiles[0].shape, 1)
    weighted = (row < 3) | (row == 7)
    total = None
    for tile, own in zip(tiles, peaks):
        scaled = jnp.where(weighted, tile * jnp.exp(own - peak), tile)
        total = scaled if total is None else total + scaled
    return jnp.where(row == 6, peak, total)


def gelu_parts(inner):
    phi = 0.5 * (1.0 + lax.erf(inner * (1.0 / math.sqrt(2.0))))
    density = jnp.exp(-0.5 * inner * inner) * (1.0 / math.sqrt(2.0 * math.pi))
    return inner * phi, phi + inner * density


def rows_to_columns(rows):
    pad = -rows.shape[0] % 8
    if pad:
        rows = jnp.concatenate([rows, jnp.zeros((pad, LANES), F32)], 0)
    return rows.T


def times_columns(cols, count, w_ref, e, lanes):
    wide = [jnp.broadcast_to(cols[:, i : i + 1], (LANES, LANES)) for i in range(count)]
    rows = []
    for j in range(lanes):
        acc = None
        for i in range(count):
            term = wide[i] * w_ref[e, LANES * i : LANES * (i + 1), LANES * j : LANES * (j + 1)]
            term = jnp.sum(term.reshape(LANES // 8, 8, LANES), 0)
            acc = term if acc is None else acc + term
        rows.append(jnp.sum(acc, 0, keepdims=True))
    return jnp.concatenate(rows, 0)


def times_rows(rows, count, w_ref, e, blocks):
    out = []
    for i in range(blocks):
        acc = None
        for j in range(count):
            term = rows[j : j + 1] * w_ref[e, LANES * i : LANES * (i + 1), LANES * j : LANES * (j + 1)]
            acc = term if acc is None else acc + term
        out.append(jnp.sum(acc.T, 0, keepdims=True))
    return jnp.concatenate(out, 0)


def front_kernel(n_dp, n_ex, x_in, ids_in, live_in, g1_in, b1_in, wqkv_in, bqv_in, wout_in, bout_in, g2_in, b2_in, keys_in,
                 cot_in, win_in, bin_in, wdown_in, bdown_in,
                 resid_out, joined_out, context_out, attn_out, logits_out, shared_out, own_out, inner_out,
                 x_ref, ids_ref, live_ref, g1_ref, b1_ref, wqkv_ref, bqv_ref, wout_ref, bout_ref, g2_ref, b2_ref, keys_ref,
                 cot_ref, win, bin_ref, wdown, bdown_ref,
                 resid_ref, joined_ref, context_ref, attn_ref, logits_ref, block_ref,
                 stats_ref, near, mine, far, got, shared_ref, own_ref, inner_ref,
                 loads, stores, send_near, recv_near, send_far, recv_far, send_out, recv_out):
    dp, ex = lax.axis_index("dp"), lax.axis_index("expert")
    owned = win.shape[0]
    all_here = greet(n_dp, n_ex, dp, ex)
    coming = load(
        (x_in, g1_in, b1_in, wqkv_in, bqv_in, ids_in, wout_in, bout_in, g2_in, b2_in, keys_in, live_in, cot_in, win_in, bin_in,
         wdown_in, bdown_in),
        (x_ref, g1_ref, b1_ref, wqkv_ref, bqv_ref, ids_ref, wout_ref, bout_ref, g2_ref, b2_ref, keys_ref, live_ref, cot_ref, win,
         bin_ref, wdown, bdown_ref), loads)
    going = []

    def keep(src, dst):
        copy = pltpu.make_async_copy(src, dst, stores.at[len(going)])
        copy.start()
        going.append(copy)

    for copy in coming[:3]:
        copy.wait()
    x = x_ref[0]
    length, width = x.shape
    hat, _ = norm_stats(x)
    normed = hat * as_row(g1_ref) + as_row(b1_ref)
    for copy in coming[3:6]:
        copy.wait()
    joined = dot(wqkv_ref[...], normed, 0, 1)
    bias = jnp.broadcast_to(bqv_ref[0:1], (8, width)).T[:, :1]
    bias_v = jnp.broadcast_to(bqv_ref[1:2], (8, width)).T[:, :1]
    scale = 1.0 / math.sqrt(HEAD_DIM)
    joined_ref[0:width] = (joined[:width] + bias) * scale
    joined_ref[width : 2 * width] = joined[width : 2 * width]
    joined_ref[2 * width :] = joined[2 * width :] + bias_v
    keep(joined_ref, joined_out)
    ids = ids_ref[...].astype(F32)
    block_ref[...] = jnp.where(column(ids) == ids, 0.0, NEGATIVE)
    half = length // 2
    for h in range(HEADS):
        at = HEAD_DIM * h
        q_hi, q_lo = parts(joined_ref[at : at + HEAD_DIM])
        k_hi, k_lo = parts(joined_ref[width + at : width + at + HEAD_DIM])
        v_hi, v_lo = parts(joined_ref[2 * width + at : 2 * width + at + HEAD_DIM])
        queries = jnp.concatenate([q_hi, q_hi, q_lo], 0)
        keys = jnp.concatenate([k_hi, k_lo, k_hi], 0).T
        values = jnp.concatenate([v_hi, v_lo], 0)
        for b in range(2):
            span = slice(half * b, half * (b + 1))
            scores = dot(keys, queries[:, span], 1, 0, None) + block_ref[:, span]
            expo = jnp.exp(scores - jnp.max(scores, 0, keepdims=True))
            attn = expo * (1.0 / jnp.sum(expo, 0, keepdims=True))
            attn_ref[h, :, span] = attn
            p_hi, p_lo = parts(attn)
            both = dot(values, p_hi, 1, 0, None)
            context_ref[at : at + HEAD_DIM, span] = both[:HEAD_DIM] + both[HEAD_DIM:] + dot(v_hi, p_lo, 1, 0, None)
        keep(attn_ref.at[h], attn_out.at[h])
    keep(context_ref, context_out)
    for copy in coming[6:13]:
        copy.wait()
    resid = x + dot(context_ref[...], wout_ref[...], 0, 0) + as_row(bout_ref)
    resid_ref[...] = resid
    keep(resid_ref, resid_out)
    hat2, _ = norm_stats(resid)
    normed2 = hat2 * as_row(g2_ref) + as_row(b2_ref)
    logits = dot(keys_ref[...], normed2, 1, 1)
    logits_ref[...] = logits
    keep(logits_ref, logits_out)
    masked = jnp.where(live_ref[...] > 0, logits, NEGATIVE)
    peak = jnp.max(masked, 1, keepdims=True)
    expo = jnp.exp(masked - peak)
    total = jnp.sum(expo, 1, keepdims=True)
    summed = dot(expo, normed2, 1, 0)
    top = jnp.max(logits, 0, keepdims=True)
    comb = jnp.exp(logits - top)
    comb = comb * (1.0 / jnp.sum(comb, 0, keepdims=True))
    part_out = dot(comb, cot_ref[0], 1, 0)
    experts = logits.shape[0]
    stats_ref[...] = to_tiles(jnp.concatenate(
        [summed, part_out, jnp.broadcast_to(peak, (experts, LANES)), jnp.broadcast_to(total, (experts, LANES))], 1))
    all_here()
    copies = []
    for i in range(1, n_ex):
        to = lax.rem(ex + i, n_ex)
        copies.append(send(stats_ref.at[pl.ds(to * owned, owned)], near.at[i - 1], send_near.at[i - 1], recv_near.at[i - 1], dp, to))
    for copy in copies:
        copy.wait()
    mine[...] = merge([stats_ref[pl.ds(ex * owned, owned)]] + [near[i] for i in range(n_ex - 1)])
    copies = []
    for i in range(1, n_dp):
        copies.append(send(mine, far.at[dp], send_far.at[i - 1], recv_far.at[i - 1], lax.rem(dp + i, n_dp), ex))
    far[dp] = mine[...]
    for copy in copies:
        copy.wait()
    tiles = merge([far[i] for i in range(n_dp)])
    for copy in coming[13:]:
        copy.wait()
    blocks, wide = win.shape[1] // LANES, win.shape[2] // LANES
    for e in range(owned):
        tile = tiles[e]
        slots = tile[0:blocks] / tile[7:8]
        d_out = tile[3 : 3 + blocks]
        bias = jnp.concatenate([bin_ref[e : e + 1, LANES * j : LANES * (j + 1)] for j in range(wide)], 0)
        inner = times_columns(rows_to_columns(slots), blocks, win, e, wide) + bias
        hidden, slope = gelu_parts(inner)
        bias = jnp.concatenate([bdown_ref[e : e + 1, LANES * j : LANES * (j + 1)] for j in range(blocks)], 0)
        out = times_columns(rows_to_columns(hidden), wide, wdown, e, blocks) + bias
        d_inner = times_rows(d_out, blocks, wdown, e, wide) * slope
        d_slots = times_rows(d_inner, wide, win, e, blocks)
        along = jnp.sum(slots * d_slots, keepdims=True)
        lane = lax.broadcasted_iota(jnp.int32, (1, LANES), 1)
        last = jnp.where(lane < LANES // 2, tile[7:8], along)
        result = jnp.concatenate([out, d_slots, tile[6:7], last], 0)
        got[e] = result
        shared_ref[ex * owned + e] = result
        own_ref[e] = jnp.concatenate([slots, d_out, jnp.zeros((2, LANES), F32)], 0)
        inner_ref[e] = jnp.concatenate([hidden, d_inner], 0)
    copies = []
    for i in range(1, n_ex):
        copies.append(send(got, shared_ref.at[pl.ds(ex * owned, owned)], send_out.at[i - 1], recv_out.at[i - 1], dp, lax.rem(ex + i, n_ex)))
    keep(own_ref, own_out)
    keep(inner_ref, inner_out)
    for copy in copies:
        copy.wait()
    keep(shared_ref, shared_out)
    for copy in going:
        copy.wait()


def norm_back(grad, hat, scale, gain):
    g = grad * gain
    return scale * (g - jnp.mean(g, -1, keepdims=True) - hat * jnp.mean(g * hat, -1, keepdims=True))


def route_kernel(live_in, wout_in, g2_in, b2_in, keys_in, cot_in, resid_in, context_in, logits_in, shared_in, own_in, inner_in,
                 act_out, dresid_out, dcontext_out, gwout_out, small_ref, gwin_out, gbin_ref, gwdown_out, gbdown_ref,
                 live_ref, wout_ref, g2_ref, b2_ref, keys_ref, cot_ref, resid_ref, context_ref, logits_ref, shared_ref, own_ref,
                 inner_ref, act_ref, dresid_ref, dcontext_ref, gwout_ref, gin, gdown, loads, stores):
    length, width = resid_ref.shape
    owned = own_ref.shape[0]
    blocks = width // LANES
    wide = gin.shape[2] // LANES
    coming = load(
        (own_in, inner_in, resid_in, shared_in, logits_in, live_in, g2_in, b2_in, keys_in, cot_in, context_in, wout_in),
        (own_ref, inner_ref, resid_ref, shared_ref, logits_ref, live_ref, g2_ref, b2_ref, keys_ref, cot_ref, context_ref, wout_ref),
        loads)
    going = []

    def keep(src, dst):
        copy = pltpu.make_async_copy(src, dst, stores.at[len(going)])
        copy.start()
        going.append(copy)

    for copy in coming[:2]:
        copy.wait()
    for e in range(owned):
        slot_cols = rows_to_columns(own_ref[e])
        hidden_cols = rows_to_columns(inner_ref[e])
        for i in range(blocks):
            col = jnp.broadcast_to(slot_cols[:, i : i + 1], (LANES, LANES))
            for j in range(wide):
                gin[e, LANES * i : LANES * (i + 1), LANES * j : LANES * (j + 1)] = col * inner_ref[e, wide + j : wide + j + 1]
        keep(gin.at[e], gwin_out.at[e])
        for j in range(wide):
            col = jnp.broadcast_to(hidden_cols[:, j : j + 1], (LANES, LANES))
            for i in range(blocks):
                gdown[e, LANES * j : LANES * (j + 1), LANES * i : LANES * (i + 1)] = col * own_ref[e, 3 + i : 4 + i]
        keep(gdown.at[e], gwdown_out.at[e])
        for j in range(wide):
            gbin_ref[e : e + 1, LANES * j : LANES * (j + 1)] = inner_ref[e, wide + j : wide + j + 1]
        for i in range(blocks):
            gbdown_ref[e : e + 1, LANES * i : LANES * (i + 1)] = own_ref[e, 3 + i : 4 + i]
    for copy in coming[2:]:
        copy.wait()
    shared = shared_ref[...]
    slot_out = from_tiles(shared, 0, 3)
    d_slots = from_tiles(shared, 3, 3)
    peak = shared[:, 6, 0:1]
    total = shared[:, 7, 0:1]
    along = shared[:, 7, LANES - 1 : LANES]
    gain = as_row(g2_ref)
    cot = cot_ref[0]
    resid = resid_ref[...]
    hat2, scale2 = norm_stats(resid)
    normed2 = hat2 * gain + as_row(b2_ref)
    logits = logits_ref[...]
    dispatch = jnp.exp(jnp.where(live_ref[...] > 0, logits, NEGATIVE) - peak) / total
    comb = jnp.exp(logits - jnp.max(logits, 0, keepdims=True))
    comb = comb * (1.0 / jnp.sum(comb, 0, keepdims=True))
    d_comb = dot(slot_out, cot, 1, 1)
    d_logits = comb * (d_comb - jnp.sum(comb * d_comb, 0, keepdims=True))
    d_logits = d_logits + dispatch * (dot(d_slots, normed2, 1, 1) - along)
    d_normed2 = dot(jnp.concatenate([dispatch, d_logits], 0), jnp.concatenate([d_slots, keys_ref[...]], 0), 0, 0)
    d_resid = cot + norm_back(d_normed2, hat2, scale2, gain)
    dresid_ref[...] = d_resid
    keep(dresid_ref, dresid_out)
    context = context_ref[...]
    gwout_ref[...] = dot(context, d_resid, 1, 0)
    keep(gwout_ref, gwout_out)
    dcontext_ref[...] = dot(wout_ref[...], d_resid, 1, 1)
    keep(dcontext_ref, dcontext_out)
    small_ref[8:16] = dot(d_logits, normed2, 1, 0)
    small_ref[4:5] = jnp.sum(d_resid, 0, keepdims=True)
    small_ref[5:6] = jnp.sum(d_normed2 * hat2, 0, keepdims=True)
    small_ref[6:7] = jnp.sum(d_normed2, 0, keepdims=True)
    small_ref[7:8] = jnp.zeros((1, width), F32)
    small_ref[0:4] = jnp.zeros((4, width), F32)
    act_ref[0] = resid + dot(comb, slot_out, 0, 0)
    keep(act_ref, act_out)
    for copy in going:
        copy.wait()


def powers(n):
    return n.bit_length() - 1


def back_kernel(n_dp, n_ex, x_in, g1_in, b1_in, wqkv_in, joined_in, context_in, attn_in, dresid_in, dcontext_in, gwout_in, small_in,
                gx_ref, grads_ref, small_ref,
                x_ref, g1_ref, b1_ref, wqkv_ref, joined_ref, context_ref, attn_ref, dresid_ref, dcontext_ref, part_ref,
                smalls, djoined_ref, normed_ref, *rest):
    halvings = 4
    boxes, rest = rest[: halvings + 1], rest[halvings + 1 :]
    mine, near, far, loads, send_sem, recv_sem, send_near, recv_near, send_far, recv_far, send_all, recv_all, local = rest
    dp, ex = lax.axis_index("dp"), lax.axis_index("expert")
    all_here = greet(n_dp, n_ex, dp, ex)
    heads = [pltpu.make_async_copy(attn_in.at[h], attn_ref.at[h], loads.at[10 + h]) for h in range(HEADS)]
    coming = load(
        (gwout_in, joined_in, dcontext_in, context_in, x_in, g1_in, b1_in, wqkv_in, dresid_in, small_in),
        (part_ref.at[0], joined_ref, dcontext_ref, context_ref, x_ref, g1_ref, b1_ref, wqkv_ref, dresid_ref, smalls), loads)
    for copy in heads:
        copy.start()
    length, width = dresid_ref.shape
    rows = part_ref.shape[1]
    bits = [("expert", 0)] + [("expert", b) for b in range(1, powers(n_ex))] + [("dp", b) for b in range(powers(n_dp))]

    def bit_of(which):
        axis, b = which
        return lax.rem((ex if axis == "expert" else dp) // (1 << b), 2)

    def flip(which, weight=1):
        axis, b = which
        step = (1 - 2 * bit_of(which)) * (1 << b) * weight
        return (0, step) if axis == "expert" else (step, 0)

    first = bit_of(bits[0])
    steps = []
    for i, which in enumerate(bits):
        if i in (1, 2):
            other = bits[3 - i]
            one, two = flip(which, 1 - first), flip(other, first)
            bit = bit_of(which) * (1 - first) + bit_of(other) * first
            steps.append((bit, (one[0] + two[0], one[1] + two[1])))
        else:
            steps.append((bit_of(which), flip(which)))
    exchanges = len(bits)
    offsets = [0]
    for i in range(halvings):
        offsets.append(pl.multiple_of(offsets[-1] + steps[i][0] * (rows >> (i + 1)), 8))
    final = rows >> halvings
    rounds = exchanges + halvings

    def launch(chunk, i):
        partner = steps[i if i < exchanges else exchanges + halvings - 1 - i][1]
        to = (dp + partner[0], ex + partner[1])
        sems = (send_sem.at[chunk, i], recv_sem.at[chunk, i])
        if i < halvings:
            size = rows >> (i + 1)
            away = pl.multiple_of(offsets[i] + (1 - steps[i][0]) * size, 8)
            src, dst = part_ref.at[chunk, pl.ds(away, size)], boxes[i].at[chunk]
        elif i < exchanges:
            src, dst = part_ref.at[chunk, pl.ds(offsets[halvings], final)], boxes[halvings].at[chunk, i - halvings]
        else:
            level = exchanges + halvings - i
            size = rows >> level
            src = dst = grads_ref.at[chunk, pl.ds(offsets[level], size)]
        return send(src, dst, *sems, *to)

    flying = {}

    def advance(chunk):
        i, copy = flying.pop(chunk)
        copy.wait()
        if i < halvings:
            size = rows >> (i + 1)
            where = pl.ds(offsets[i + 1], size)
            part_ref[chunk, where] = part_ref[chunk, where] + boxes[i][chunk]
        elif i < exchanges:
            where = pl.ds(offsets[halvings], final)
            total = part_ref[chunk, where] + boxes[halvings][chunk, i - halvings]
            if i < exchanges - 1:
                part_ref[chunk, where] = total
            else:
                grads_ref[chunk, where] = total
        if i + 1 < rounds:
            flying[chunk] = (i + 1, launch(chunk, i + 1))

    def begin(chunk):
        flying[chunk] = (0, launch(chunk, 0))

    coming[0].wait()
    all_here()
    begin(0)
    for copy in coming[1:7] + coming[9:]:
        copy.wait()
    x = x_ref[0]
    hat, scale1 = norm_stats(x)
    gain = as_row(g1_ref)
    normed_ref[0:width] = (hat * gain + as_row(b1_ref)).T
    normed_ref[width:] = jnp.ones((8, length), F32)
    scale = 1.0 / math.sqrt(HEAD_DIM)
    half = length // 2
    d_normed = None
    pair = 2 * HEAD_DIM
    for h in range(HEADS):
        at = HEAD_DIM * h
        span = slice(at, at + HEAD_DIM)
        q_hi, q_lo = parts(joined_ref[at : at + HEAD_DIM])
        k_hi, k_lo = parts(joined_ref[width + at : width + at + HEAD_DIM])
        v_hi, v_lo = parts(joined_ref[2 * width + at : 2 * width + at + HEAD_DIM])
        d_context = dcontext_ref[span]
        o_hi, o_lo = parts(d_context)
        rowsum = jnp.sum(d_context * context_ref[span], 0, keepdims=True)
        values = jnp.concatenate([v_hi, v_lo, v_hi], 0).T
        d_out = jnp.concatenate([o_hi, o_hi, o_lo], 0)
        keys = jnp.concatenate([k_hi, k_lo], 0)
        queries = jnp.concatenate([q_hi, q_lo], 0)
        outs = jnp.concatenate([o_hi, o_lo], 0)
        heads[h].wait()
        d_v = d_k = None
        for b in range(2):
            part = slice(half * b, half * (b + 1))
            attn = attn_ref[h, :, part]
            d_attn = dot(values, d_out[:, part], 1, 0, None)
            d_scores = attn * (d_attn - rowsum[:, part])
            p_hi, p_lo = parts(attn)
            s_hi, s_lo = parts(d_scores)
            both = dot(keys, s_hi, 1, 0, None)
            d_q = both[:HEAD_DIM] + both[HEAD_DIM:] + dot(k_hi, s_lo, 1, 0, None)
            djoined_ref[at : at + HEAD_DIM, part] = d_q * scale
            both = dot(outs[:, part], p_hi, 1, 1, None)
            term = both[:HEAD_DIM] + both[HEAD_DIM:] + dot(o_hi[:, part], p_lo, 1, 1, None)
            d_v = term if d_v is None else d_v + term
            both = dot(queries[:, part], s_hi, 1, 1, None)
            term = both[:HEAD_DIM] + both[HEAD_DIM:] + dot(q_hi[:, part], s_lo, 1, 1, None)
            d_k = term if d_k is None else d_k + term
        djoined_ref[width + at : width + at + HEAD_DIM] = d_k
        djoined_ref[2 * width + at : 2 * width + at + HEAD_DIM] = d_v
        for chunk in sorted(flying):
            advance(chunk)
        if h % 2:
            p = h // 2
            spans = [slice(t * width + pair * p, t * width + pair * (p + 1)) for t in range(3)]
            d_part = jnp.concatenate([djoined_ref[s] for s in spans], 0)
            grad = dot(normed_ref[...], d_part, 1, 1)
            part_ref[1 + p] = grad[:width]
            begin(1 + p)
            smalls[2:3, pair * p : pair * (p + 1)] = grad[width : width + 1, :pair]
            smalls[3:4, pair * p : pair * (p + 1)] = grad[width : width + 1, 2 * pair :]
    coming[7].wait()
    d_normed = dot(djoined_ref[...], wqkv_ref[...], 0, 1)
    coming[8].wait()
    smalls[0:1] = jnp.sum(d_normed * hat, 0, keepdims=True)
    smalls[1:2] = jnp.sum(d_normed, 0, keepdims=True)
    for chunk in sorted(flying):
        advance(chunk)
    count = width // LANES
    everything = jnp.concatenate([smalls[:, LANES * i : LANES * (i + 1)] for i in range(count)], 0)
    share = mine.shape[1]
    pad = n_ex * share - everything.shape[0]
    everything = jnp.concatenate([everything, jnp.zeros((pad, LANES), F32)], 0)
    for i in range(n_ex):
        mine[i] = everything[share * i : share * (i + 1)]
    copies = []
    for i in range(1, n_ex):
        to = lax.rem(ex + i, n_ex)
        copies.append(send(mine.at[to], near.at[i - 1], send_near.at[i - 1], recv_near.at[i - 1], dp, to))
    gx_ref[0] = dresid_ref[...] + norm_back(d_normed, hat, scale1, gain)
    for copy in copies:
        copy.wait()
    local[0] = functools.reduce(jnp.add, [mine[ex]] + [near[i] for i in range(n_ex - 1)])
    copies = []
    for i in range(1, n_dp):
        copies.append(send(local.at[0], far.at[dp], send_far.at[i - 1], recv_far.at[i - 1], lax.rem(dp + i, n_dp), ex))
    far[dp] = local[0]
    for chunk in sorted(flying):
        advance(chunk)
    for copy in copies:
        copy.wait()
    total = functools.reduce(jnp.add, [far[i] for i in range(n_dp)])
    local[1] = total
    copies = []
    for i in range(1, n_ex):
        copies.append(send(local.at[1], small_ref.at[ex], send_all.at[i - 1], recv_all.at[i - 1], dp, lax.rem(ex + i, n_ex)))
    small_ref[ex] = total
    while flying:
        for chunk in sorted(flying):
            advance(chunk)
    for copy in copies:
        copy.wait()


def finish_kernel(grads_in, small_ref, gx_in, gx_out, g1_ref, b1_ref, gwqkv_out, gbqv_ref, gwout_out, gbout_ref, g2_ref, b2_ref,
                  gkeys_ref, grads_ref, gx_ref, sems):
    width = grads_in.shape[1]
    pair = 2 * HEAD_DIM
    coming = load([grads_in.at[i] for i in range(grads_in.shape[0])] + [gx_in],
                  [grads_ref.at[i] for i in range(grads_in.shape[0])] + [gx_ref], sems)
    flat = small_ref[...].reshape(-1, LANES)
    count = width // LANES
    rows = jnp.concatenate([flat[16 * i : 16 * (i + 1)] for i in range(count)], 1)
    for ref, i in ((g1_ref, 0), (b1_ref, 1), (gbout_ref, 4), (g2_ref, 5), (b2_ref, 6)):
        ref[...] = rows[i : i + 1].reshape(width)
    gbqv_ref[...] = rows[2:4]
    gkeys_ref[...] = rows[8:16]
    going = []

    def keep(src, dst):
        copy = pltpu.make_async_copy(src, dst, sems.at[len(coming) + len(going)])
        copy.start()
        going.append(copy)

    coming[0].wait()
    keep(grads_ref.at[0], gwout_out)
    for p in range(HEADS // 2):
        coming[1 + p].wait()
        for t in range(3):
            keep(grads_ref.at[1 + p, :, pl.ds(pair * t, pair)], gwqkv_out.at[:, pl.ds(t * width + pair * p, pair)])
    coming[-1].wait()
    keep(gx_ref, gx_out)
    for copy in going:
        copy.wait()


def sds(*shape):
    return jax.ShapeDtypeStruct(shape, F32)


def vm(*shape):
    return pltpu.VMEM(shape, F32)


def dma(*shape):
    return pltpu.SemaphoreType.DMA(shape)


def solution(mesh):
    n_dp, n_ex = mesh.shape["dp"], mesh.shape["expert"]

    def on_device(patches, image_ids, pad_mask, ln1_gain, ln1_bias, w_qkv, bias_qv, w_out, bias_out, ln2_gain, ln2_bias,
                  slot_keys, w_in, bias_in, w_down, bias_down, cotangent):
        _, length, width = patches.shape
        owned, _, hidden = w_in.shape
        experts = owned * n_ex
        wide = hidden // LANES
        keys_t = slot_keys.T
        like = lambda *arrays: [pltpu.VMEM(a.shape, a.dtype) for a in arrays]
        args = (patches, image_ids, pad_mask, ln1_gain, ln1_bias, w_qkv, bias_qv, w_out, bias_out, ln2_gain, ln2_bias, keys_t,
                cotangent, w_in, bias_in, w_down, bias_down)
        resid, joined, context, attn, logits, shared, own, inner = pl.pallas_call(
            functools.partial(front_kernel, n_dp, n_ex),
            out_shape=(sds(length, width), sds(3 * width, length), sds(width, length), sds(HEADS, length, length),
                       sds(experts, length), sds(experts, 8, LANES), sds(owned, 8, LANES), sds(owned, 2 * wide, LANES)),
            in_specs=[ANY] * len(args),
            out_specs=[ANY] * 8,
            scratch_shapes=like(*args) + [
                vm(length, width), vm(3 * width, length), vm(width, length), vm(HEADS, length, length), vm(experts, length),
                vm(length, length), vm(experts, 8, LANES), vm(n_ex - 1, owned, 8, LANES), vm(owned, 8, LANES),
                vm(n_dp, owned, 8, LANES), vm(owned, 8, LANES), vm(experts, 8, LANES), vm(owned, 8, LANES),
                vm(owned, 2 * wide, LANES), dma(len(args)), dma(HEADS + 7), dma(n_ex - 1), dma(n_ex - 1), dma(n_dp - 1),
                dma(n_dp - 1), dma(n_ex - 1), dma(n_ex - 1)],
            compiler_params=pltpu.CompilerParams(collective_id=0, has_side_effects=True, vmem_limit_bytes=FRONT_VMEM),
            name="front",
        )(*args)
        args = (pad_mask, w_out, ln2_gain, ln2_bias, keys_t, cotangent, resid, context, logits, shared, own, inner)
        act, d_resid, d_context, gwout, small, gwin, gbin, gwdown, gbdown = pl.pallas_call(
            route_kernel,
            out_shape=(sds(1, length, width), sds(length, width), sds(width, length), sds(width, width), sds(16, width),
                       sds(*w_in.shape), sds(*bias_in.shape), sds(*w_down.shape), sds(*bias_down.shape)),
            in_specs=[ANY] * len(args),
            out_specs=[ANY] * 4 + [VMEM, ANY, VMEM, ANY, VMEM],
            scratch_shapes=like(*args) + [vm(1, length, width), vm(length, width), vm(width, length), vm(width, width),
                                          vm(*w_in.shape), vm(*w_down.shape), dma(len(args)), dma(2 * owned + 4)],
            compiler_params=pltpu.CompilerParams(vmem_limit_bytes=ROUTE_VMEM),
            name="route",
        )(*args)
        chunks = 1 + HEADS // 2
        halvings = 4
        rounds = powers(n_dp) + powers(n_ex) + halvings
        share = 16
        args = (patches, ln1_gain, ln1_bias, w_qkv, joined, context, attn, d_resid, d_context, gwout, small)
        gx, grads, small = pl.pallas_call(
            functools.partial(back_kernel, n_dp, n_ex),
            out_shape=(sds(1, length, width), sds(chunks, width, width), sds(n_ex, share, LANES)),
            in_specs=[ANY] * len(args),
            out_specs=[VMEM] * 3,
            scratch_shapes=like(*args[:9]) + [vm(chunks, width, width), vm(16, width), vm(3 * width, length), vm(width + 8, length)]
            + [vm(chunks, width >> (i + 1), width) for i in range(halvings)]
            + [vm(chunks, rounds - 2 * halvings, width >> halvings, width), vm(n_ex, share, LANES), vm(n_ex - 1, share, LANES),
               vm(n_dp, share, LANES), dma(10 + HEADS), dma(chunks, rounds), dma(chunks, rounds), dma(n_ex - 1), dma(n_ex - 1),
               dma(n_dp - 1), dma(n_dp - 1), dma(n_ex - 1), dma(n_ex - 1), vm(2, share, LANES)],
            compiler_params=pltpu.CompilerParams(collective_id=1, has_side_effects=True, vmem_limit_bytes=BACK_VMEM),
            name="back",
        )(*args)
        gx, g1, b1, gwqkv, gbqv, gwout, gbout, g2, b2, gkeys = pl.pallas_call(
            finish_kernel,
            out_shape=(sds(1, length, width), sds(width), sds(width), sds(*w_qkv.shape), sds(*bias_qv.shape), sds(*w_out.shape),
                       sds(width), sds(width), sds(width), sds(experts, width)),
            in_specs=[ANY, VMEM, ANY],
            out_specs=[ANY, VMEM, VMEM, ANY, VMEM, ANY, VMEM, VMEM, VMEM, VMEM],
            scratch_shapes=[vm(chunks, width, width), vm(1, length, width), dma(2 * chunks + 2 + 3 * chunks)],
            compiler_params=pltpu.CompilerParams(vmem_limit_bytes=FINISH_VMEM),
            name="finish",
        )(grads, small, gx)
        return (act, gx, g1, b1, gwqkv, gbqv, gwout, gbout, g2, b2, gkeys.T, gwin, gbin, gwdown, gbdown)

    rows = P(("dp", "expert"), None, None)
    flags = P(("dp", "expert"), None)
    e3, e2 = P("expert", None, None), P("expert", None)
    return jax.shard_map(
        on_device,
        mesh=mesh,
        in_specs=(rows, flags, flags) + (P(),) * 9 + (e3, e2, e3, e2, rows),
        out_specs=(rows, rows) + (P(),) * 9 + (e3, e2, e3, e2),
        check_vma=False,
    )
```

```python
import functools
import math

import jax
import jax.numpy as jnp
from jax import lax
from jax.experimental import pallas as pl
from jax.experimental.pallas import tpu as pltpu
from jax.sharding import PartitionSpec as P

HEADS = 6
HEAD_DIM = 64
LANES = 128
EPSILON = 1e-06
NEGATIVE = -1e30
HIGH = lax.Precision.HIGH
BF = jnp.bfloat16
F32 = jnp.float32
MESH = pl.DeviceIdType.MESH
LAYER_VMEM = 56 << 20
FINISH_VMEM = 56 << 20
PLAN = {
    "kinds": ('direct', 'direct', 'direct', 'direct', 'direct', 'direct', 'small'),
    "ticks": {3: (0,), 10: (1,), 12: (0,), 13: (2,), 17: (3,), 18: (1,), 19: (4, 2), 20: (5,)},
    "drain": (0, 3, 6, 4, 5, 1, 0, 0, 2, 1, 3, 1, 6, 2, 4, 2, 5, 6, 3, 3, 4, 4, 5, 5),
}
VMEM = pl.BlockSpec(memory_space=pltpu.VMEM)
ANY = pl.BlockSpec(memory_space=pl.ANY)


def dot(left, right, dim_left, dim_right, precision=HIGH):
    return lax.dot_general(
        left, right, (((dim_left,), (dim_right,)), ((), ())), precision=precision, preferred_element_type=F32
    )


def parts(value):
    high = value.astype(BF)
    return high, (value - high.astype(F32)).astype(BF)


def norm_stats(values):
    center = values - jnp.mean(values, -1, keepdims=True)
    spread = jnp.mean(center * center, -1, keepdims=True)
    scale = lax.rsqrt(spread + EPSILON)
    return center * scale, scale


def column(row):
    return jnp.broadcast_to(row, (8, row.shape[1])).T[:, :1]


def load(sources, targets, sems):
    copies = [pltpu.make_async_copy(src, dst, sems.at[i]) for i, (src, dst) in enumerate(zip(sources, targets))]
    for copy in copies:
        copy.start()
    return copies


def greet(n_dp, n_ex, dp, ex):
    barrier = pltpu.get_barrier_semaphore()
    for i in range(1, n_ex):
        pl.semaphore_signal(barrier, inc=1, device_id=(dp, lax.rem(ex + i, n_ex)), device_id_type=MESH)
    for i in range(1, n_dp):
        pl.semaphore_signal(barrier, inc=1, device_id=(lax.rem(dp + i, n_dp), ex), device_id_type=MESH)
    return lambda: pl.semaphore_wait(barrier, n_ex + n_dp - 2)


def send(src, dst, out_sem, in_sem, dp, ex):
    copy = pltpu.make_async_remote_copy(
        src_ref=src, dst_ref=dst, send_sem=out_sem, recv_sem=in_sem, device_id=(dp, ex), device_id_type=MESH)
    copy.start()
    return copy


def as_row(ref):
    return ref[...].reshape(1, -1)


def to_tiles(rows):
    return jnp.stack([jnp.concatenate([rows[e : e + 1, LANES * i : LANES * (i + 1)] for i in range(8)], 0) for e in range(rows.shape[0])], 0)


def from_tiles(tiles, first, count):
    return jnp.concatenate([tiles[:, first + i, :] for i in range(count)], -1)


def merge(tiles):
    peaks = [tile[:, 6:7, :] for tile in tiles]
    peak = functools.reduce(jnp.maximum, peaks)
    row = lax.broadcasted_iota(jnp.int32, tiles[0].shape, 1)
    weighted = (row < 3) | (row == 7)
    total = None
    for tile, own in zip(tiles, peaks):
        scaled = jnp.where(weighted, tile * jnp.exp(own - peak), tile)
        total = scaled if total is None else total + scaled
    return jnp.where(row == 6, peak, total)


def gelu_parts(inner):
    phi = 0.5 * (1.0 + lax.erf(inner * (1.0 / math.sqrt(2.0))))
    density = jnp.exp(-0.5 * inner * inner) * (1.0 / math.sqrt(2.0 * math.pi))
    return inner * phi, phi + inner * density


def rows_to_columns(rows):
    pad = -rows.shape[0] % 8
    if pad:
        rows = jnp.concatenate([rows, jnp.zeros((pad, LANES), F32)], 0)
    return rows.T


def times_columns(cols, count, w_ref, e, lanes):
    wide = [jnp.broadcast_to(cols[:, i : i + 1], (LANES, LANES)) for i in range(count)]
    rows = []
    for j in range(lanes):
        acc = None
        for i in range(count):
            term = wide[i] * w_ref[e, LANES * i : LANES * (i + 1), LANES * j : LANES * (j + 1)]
            term = jnp.sum(term.reshape(LANES // 8, 8, LANES), 0)
            acc = term if acc is None else acc + term
        rows.append(jnp.sum(acc, 0, keepdims=True))
    return jnp.concatenate(rows, 0)


def times_rows(rows, count, w_ref, e, blocks):
    out = []
    for i in range(blocks):
        acc = None
        for j in range(count):
            term = rows[j : j + 1] * w_ref[e, LANES * i : LANES * (i + 1), LANES * j : LANES * (j + 1)]
            acc = term if acc is None else acc + term
        out.append(jnp.sum(acc.T, 0, keepdims=True))
    return jnp.concatenate(out, 0)


def norm_back(grad, hat, scale, gain):
    g = grad * gain
    return scale * (g - jnp.mean(g, -1, keepdims=True) - hat * jnp.mean(g * hat, -1, keepdims=True))


def powers(n):
    return n.bit_length() - 1


HALVINGS = 4
INPUTS = ("x", "g1", "b1", "wqkv", "bqv", "ids", "wout", "bout", "g2", "b2", "keys", "live", "cot", "win", "bin", "wdown", "bdown")


def layer_kernel(n_dp, n_ex, names, *refs):
    at = dict(zip(names, refs))
    dp, ex = lax.axis_index("dp"), lax.axis_index("expert")
    stats_ref, near, mine, far, got, shared_ref, own_ref, inner_ref = (
        at[n] for n in ("stats", "near", "mine", "far", "got", "shared", "own", "inner"))
    win, wdown, bin_ref, bdown_ref = at["win"], at["wdown"], at["bin"], at["bdown"]
    joined_ref, context_ref, attn_ref, block_ref = at["joined"], at["context"], at["attn"], at["block"]
    high_ref, low_ref, kk_ref, qq_ref, vt_ref = at["high"], at["low"], at["kk"], at["qq"], at["vt"]
    djoined_ref, normed_ref, smalls = at["djoined"], at["normed"], at["smalls"]
    sems = at["sems"]
    owned = win.shape[0]
    all_here = greet(n_dp, n_ex, dp, ex)
    coming = dict(zip(INPUTS, load([at[n + "_in"] for n in INPUTS], [at[n] for n in INPUTS], at["loads"])))

    def ready(*which):
        for n in which:
            coming[n].wait()

    ready("x", "g1", "b1")
    x = at["x"][0]
    length, width = x.shape
    half = length // 2
    halves = [slice(half * b, half * (b + 1)) for b in range(2)]
    hat, _ = norm_stats(x)
    normed = hat * as_row(at["g1"]) + as_row(at["b1"])
    ready("wqkv", "bqv", "ids")
    joined = dot(at["wqkv"][...], normed, 0, 1)
    bias = jnp.broadcast_to(at["bqv"][0:1], (8, width)).T[:, :1]
    bias_v = jnp.broadcast_to(at["bqv"][1:2], (8, width)).T[:, :1]
    scale = 1.0 / math.sqrt(HEAD_DIM)
    joined_ref[0:width] = (joined[:width] + bias) * scale
    joined_ref[width : 2 * width] = joined[width : 2 * width]
    joined_ref[2 * width :] = joined[2 * width :] + bias_v
    ids = at["ids"][...].astype(F32)
    block_ref[...] = jnp.where(column(ids) == ids, 0.0, NEGATIVE)
    for h in range(HEADS):
        lo = HEAD_DIM * h
        q_hi, q_lo = parts(joined_ref[lo : lo + HEAD_DIM])
        k_hi, k_lo = parts(joined_ref[width + lo : width + lo + HEAD_DIM])
        v_hi, v_lo = parts(joined_ref[2 * width + lo : 2 * width + lo + HEAD_DIM])
        queries = jnp.concatenate([q_hi, q_hi, q_lo], 0)
        keys = jnp.concatenate([k_hi, k_lo, k_hi], 0).T
        values = jnp.concatenate([v_hi, v_lo], 0)
        kk_ref[h] = jnp.concatenate([k_hi, k_lo], 0)
        qq_ref[h] = jnp.concatenate([q_hi, q_lo], 0)
        vt_ref[h] = values
        for part in halves:
            scores = dot(keys, queries[:, part], 1, 0, None) + block_ref[:, part]
            expo = jnp.exp(scores - jnp.max(scores, 0, keepdims=True))
            attn = expo * (1.0 / jnp.sum(expo, 0, keepdims=True))
            attn_ref[h, :, part] = attn
            p_hi, p_lo = parts(attn)
            high_ref[h, :, part] = p_hi
            low_ref[h, :, part] = p_lo
            both = dot(values, p_hi, 1, 0, None)
            context_ref[lo : lo + HEAD_DIM, part] = both[:HEAD_DIM] + both[HEAD_DIM:] + dot(v_hi, p_lo, 1, 0, None)
    ready("wout", "bout", "g2", "b2", "keys", "live", "cot")
    context = context_ref[...]
    resid = x + dot(context, at["wout"][...], 0, 0) + as_row(at["bout"])
    gain2 = as_row(at["g2"])
    hat2, scale2 = norm_stats(resid)
    normed2 = hat2 * gain2 + as_row(at["b2"])
    logits = dot(at["keys"][...], normed2, 1, 1)
    masked = jnp.where(at["live"][...] > 0, logits, NEGATIVE)
    peak = jnp.max(masked, 1, keepdims=True)
    expo = jnp.exp(masked - peak)
    total = jnp.sum(expo, 1, keepdims=True)
    summed = dot(expo, normed2, 1, 0)
    comb = jnp.exp(logits - jnp.max(logits, 0, keepdims=True))
    comb = comb * (1.0 / jnp.sum(comb, 0, keepdims=True))
    cot = at["cot"][0]
    part_out = dot(comb, cot, 1, 0)
    experts = logits.shape[0]
    stats_ref[...] = to_tiles(jnp.concatenate(
        [summed, part_out, jnp.broadcast_to(peak, (experts, LANES)), jnp.broadcast_to(total, (experts, LANES))], 1))
    all_here()
    copies = []
    for i in range(1, n_ex):
        to = lax.rem(ex + i, n_ex)
        copies.append(send(stats_ref.at[pl.ds(to * owned, owned)], near.at[i - 1], sems.at[0, 0, i], sems.at[1, 0, i], dp, to))
    normed_ref[0:width] = normed.T
    normed_ref[width:] = jnp.ones((8, length), F32)
    for copy in copies:
        copy.wait()
    mine[...] = merge([stats_ref[pl.ds(ex * owned, owned)]] + [near[i] for i in range(n_ex - 1)])
    copies = []
    for i in range(1, n_dp):
        copies.append(send(mine, far.at[dp], sems.at[0, 1, i], sems.at[1, 1, i], lax.rem(dp + i, n_dp), ex))
    far[dp] = mine[...]
    ready("win", "bin", "wdown", "bdown")
    for copy in copies:
        copy.wait()
    tiles = merge([far[i] for i in range(n_dp)])
    blocks, wide = win.shape[1] // LANES, win.shape[2] // LANES
    for e in range(owned):
        tile = tiles[e]
        slots = tile[0:blocks] / tile[7:8]
        d_out = tile[3 : 3 + blocks]
        bias = jnp.concatenate([bin_ref[e : e + 1, LANES * j : LANES * (j + 1)] for j in range(wide)], 0)
        inner = times_columns(rows_to_columns(slots), blocks, win, e, wide) + bias
        hidden, slope = gelu_parts(inner)
        bias = jnp.concatenate([bdown_ref[e : e + 1, LANES * j : LANES * (j + 1)] for j in range(blocks)], 0)
        out = times_columns(rows_to_columns(hidden), wide, wdown, e, blocks) + bias
        d_inner = times_rows(d_out, blocks, wdown, e, wide) * slope
        d_slots = times_rows(d_inner, wide, win, e, blocks)
        along = jnp.sum(slots * d_slots, keepdims=True)
        lane = lax.broadcasted_iota(jnp.int32, (1, LANES), 1)
        last = jnp.where(lane < LANES // 2, tile[7:8], along)
        result = jnp.concatenate([out, d_slots, tile[6:7], last], 0)
        got[e] = result
        shared_ref[ex * owned + e] = result
        own_ref[e] = jnp.concatenate([slots, d_out, jnp.zeros((2, LANES), F32)], 0)
        inner_ref[e] = jnp.concatenate([hidden, d_inner], 0)
    copies = []
    for i in range(1, n_ex):
        copies.append(send(got, shared_ref.at[pl.ds(ex * owned, owned)], sems.at[0, 2, i], sems.at[1, 2, i], dp, lax.rem(ex + i, n_ex)))
    for copy in copies:
        copy.wait()

    bits = [("expert", 0)] + [("expert", b) for b in range(1, powers(n_ex))] + [("dp", b) for b in range(powers(n_dp))]

    def bit_of(which):
        axis, b = which
        return lax.rem((ex if axis == "expert" else dp) // (1 << b), 2)

    def flip(which, weight=1):
        axis, b = which
        step = (1 - 2 * bit_of(which)) * (1 << b) * weight
        return (0, step) if axis == "expert" else (step, 0)

    first = bit_of(bits[0])
    steps = []
    for i, which in enumerate(bits):
        if i in (1, 2):
            other = bits[3 - i]
            one, two = flip(which, 1 - first), flip(other, first)
            bit = bit_of(which) * (1 - first) + bit_of(other) * first
            steps.append((bit, (one[0] + two[0], one[1] + two[1])))
        else:
            steps.append((bit_of(which), flip(which)))
    exchanges = len(bits)

    def halving(chunk):
        part, total, *boxes, send_sem, recv_sem = chunk
        rows = part.shape[0]
        offsets = [0]
        for i in range(HALVINGS):
            offsets.append(pl.multiple_of(offsets[-1] + steps[i][0] * (rows >> (i + 1)), 8))
        final = pl.ds(offsets[HALVINGS], rows >> HALVINGS)

        def start(i):
            partner = steps[i if i < exchanges else exchanges + HALVINGS - 1 - i][1]
            if i < HALVINGS:
                size = rows >> (i + 1)
                away = pl.multiple_of(offsets[i] + (1 - steps[i][0]) * size, 8)
                src, dst = part.at[pl.ds(away, size)], boxes[i]
            elif i < exchanges:
                src, dst = part.at[final], boxes[HALVINGS].at[i - HALVINGS]
            else:
                level = exchanges + HALVINGS - i
                src = dst = total.at[pl.ds(offsets[level], rows >> level)]
            return [send(src, dst, send_sem.at[i], recv_sem.at[i], dp + partner[0], ex + partner[1])]

        def absorb(i):
            if i < HALVINGS:
                where = pl.ds(offsets[i + 1], rows >> (i + 1))
                part[where] = part[where] + boxes[i][...]
            elif i < exchanges - 1:
                part[final] = part[final] + boxes[HALVINGS][i - HALVINGS]
            elif i == exchanges - 1:
                total[final] = part[final] + boxes[HALVINGS][i - HALVINGS]

        return start, absorb, exchanges + HALVINGS

    x_bit, y_bit = bit_of(("expert", 1)), bit_of(("dp", 0))
    deep, n_deep = dp // 2, n_dp // 2

    def direct(chunk):
        part, total, box_core, box_plane, box_deep, wires = chunk
        rows = part.shape[0]
        half, quarter = rows // 2, rows // 8
        base = pl.multiple_of(first * half, 8)
        away = pl.multiple_of((1 - first) * half, 8)

        def spot(j):
            flip_x, flip_y = j % 2, j // 2
            to_x = x_bit + (1 - 2 * x_bit) * flip_x
            to_y = y_bit + (1 - 2 * y_bit) * flip_y
            row = pl.multiple_of(base + quarter * (to_x + 2 * to_y), 8)
            return pl.ds(row, quarter), dp + (to_y - y_bit), ex + 2 * (to_x - x_bit)

        own = spot(0)[0]

        def start(i):
            if i in (0, 4):
                core = (dp, ex + 1 - 2 * first)
                src, dst = (part.at[pl.ds(away, half)], box_core) if i == 0 else (total.at[pl.ds(base, half)],) * 2
                return [send(src, dst, wires.at[0, i], wires.at[1, i], *core)]
            copies = []
            if i == 2:
                for k in range(1, n_deep):
                    copies.append(send(part.at[own], box_deep.at[deep], wires.at[0, 10 + k], wires.at[1, 10 + k], lax.rem(dp + 2 * k, n_dp), ex))
                box_deep[deep] = part[own]
            else:
                for j in range(1, 4):
                    where, to_dp, to_ex = spot(j)
                    src, dst = (part.at[where], box_plane.at[j - 1]) if i == 1 else (total.at[own],) * 2
                    at = (4 if i == 1 else 7) + j
                    copies.append(send(src, dst, wires.at[0, at], wires.at[1, at], to_dp, to_ex))
            return copies

        def absorb(i):
            if i == 0:
                part[pl.ds(base, half)] = part[pl.ds(base, half)] + box_core[...]
            elif i == 1:
                part[own] = (part[own] + box_plane[0]) + (box_plane[1] + box_plane[2])
            elif i == 2:
                total[own] = functools.reduce(jnp.add, [box_deep[k] for k in range(n_deep)])

        return start, absorb, 5

    def small(chunk):
        to_near, from_near, from_far, local, result = chunk

        def start(i):
            copies = []
            if i == 1:
                for k in range(1, n_dp):
                    copies.append(send(local.at[0], from_far.at[dp], sems.at[0, 4, k], sems.at[1, 4, k], lax.rem(dp + k, n_dp), ex))
                from_far[dp] = local[0]
                return copies
            for k in range(1, n_ex):
                to = lax.rem(ex + k, n_ex)
                src, dst = (to_near.at[to], from_near.at[k - 1]) if i == 0 else (local.at[1], result.at[ex])
                copies.append(send(src, dst, sems.at[0, 3 + i, k], sems.at[1, 3 + i, k], dp, to))
            if i == 2:
                result[ex] = local[1]
            return copies

        def absorb(i):
            if i == 0:
                local[0] = functools.reduce(jnp.add, [to_near[ex]] + [from_near[k] for k in range(n_ex - 1)])
            elif i == 1:
                local[1] = functools.reduce(jnp.add, [from_far[k] for k in range(n_dp)])

        return start, absorb, 3

    kinds = {"halving": halving, "direct": direct, "small": small}
    chunks = [[at[f"c{c}_{i}"] for i in range(sum(n.startswith(f"c{c}_") for n in names))] for c in range(len(PLAN["kinds"]))]
    flying = {}
    slot = [0]

    def begin(c):
        start, absorb, rounds = kinds[PLAN["kinds"][c]](chunks[c])
        flying[c] = [start, absorb, rounds, 0, start(0)]

    def advance(c):
        if c not in flying:
            return
        start, absorb, rounds, i, copies = flying[c]
        for copy in copies:
            copy.wait()
        absorb(i)
        if i + 1 < rounds:
            flying[c][3:] = [i + 1, start(i + 1)]
        else:
            del flying[c]

    def tick():
        for c in PLAN["ticks"].get(slot[0], ()):
            advance(c)
        slot[0] += 1

    shared = shared_ref[...]
    slot_out = from_tiles(shared, 0, 3)
    d_slots = from_tiles(shared, 3, 3)
    peak = shared[:, 6, 0:1]
    total = shared[:, 7, 0:1]
    along = shared[:, 7, LANES - 1 : LANES]
    dispatch = jnp.exp(masked - peak) / total
    d_comb = dot(slot_out, cot, 1, 1)
    d_logits = comb * (d_comb - jnp.sum(comb * d_comb, 0, keepdims=True))
    d_logits = d_logits + dispatch * (dot(d_slots, normed2, 1, 1) - along)
    d_normed2 = dot(jnp.concatenate([dispatch, d_logits], 0), jnp.concatenate([d_slots, at["keys"][...]], 0), 0, 0)
    d_resid = cot + norm_back(d_normed2, hat2, scale2, gain2)
    chunks[0][0][...] = dot(context_ref[...], d_resid, 1, 0)
    begin(0)
    d_context = dot(at["wout"][...], d_resid, 1, 1)
    tick()
    outs = []
    for h in range(HEADS):
        lo = HEAD_DIM * h
        o_hi, o_lo = parts(d_context[lo : lo + HEAD_DIM])
        outs.append((o_hi, o_lo))
        both = jnp.concatenate([o_hi, o_lo], 0)
        d_v = None
        for part in halves:
            high = dot(both[:, part], high_ref[h, :, part], 1, 1, None)
            term = high[:HEAD_DIM] + high[HEAD_DIM:] + dot(o_hi[:, part], low_ref[h, :, part], 1, 1, None)
            d_v = term if d_v is None else d_v + term
        djoined_ref[2 * width + lo : 2 * width + lo + HEAD_DIM] = d_v
        tick()
    grad = dot(normed_ref[...], djoined_ref[2 * width :], 1, 1)
    chunks[1][0][...] = grad[:width]
    begin(1)
    smalls[3:4] = grad[width : width + 1]
    launch_at = {1: (2, 0, 2), 3: (3, 2, 4), 4: (4, 4, 5), 5: (5, 5, 6)}
    for h in range(HEADS):
        lo = HEAD_DIM * h
        span = slice(lo, lo + HEAD_DIM)
        o_hi, o_lo = outs[h]
        rowsum = jnp.sum(d_context[span] * context_ref[span], 0, keepdims=True)
        v_both, keys, queries = vt_ref[h], kk_ref[h], qq_ref[h]
        values = jnp.concatenate([v_both, v_both[:HEAD_DIM]], 0).T
        d_out = jnp.concatenate([o_hi, o_hi, o_lo], 0)
        d_k = None
        for part in halves:
            d_attn = dot(values, d_out[:, part], 1, 0, None)
            s_hi, s_lo = parts(attn_ref[h, :, part] * (d_attn - rowsum[:, part]))
            both = dot(keys, s_hi, 1, 0, None)
            d_q = both[:HEAD_DIM] + both[HEAD_DIM:] + dot(keys[:HEAD_DIM], s_lo, 1, 0, None)
            djoined_ref[span, part] = d_q * scale
            both = dot(queries[:, part], s_hi, 1, 1, None)
            term = both[:HEAD_DIM] + both[HEAD_DIM:] + dot(queries[:HEAD_DIM, part], s_lo, 1, 1, None)
            d_k = term if d_k is None else d_k + term
            tick()
        djoined_ref[width + lo : width + lo + HEAD_DIM] = d_k
        if h in launch_at:
            c, lo, hi = launch_at[h]
            lo, hi = lo * HEAD_DIM, hi * HEAD_DIM
            d_part = jnp.concatenate([djoined_ref[lo:hi], djoined_ref[width + lo : width + hi]], 0)
            grad = dot(normed_ref[...], d_part, 1, 1)
            chunks[c][0][...] = grad[:width]
            begin(c)
            row = grad[width : width + 1, : hi - lo]
            if (hi - lo) % LANES == 0:
                smalls[2:3, lo:hi] = row
            elif lo % LANES == 0:
                kept_row = row
            else:
                smalls[2:3, lo - HEAD_DIM : hi] = jnp.concatenate([kept_row, row], 1)
    d_normed = dot(djoined_ref[...], at["wqkv"][...], 0, 1)
    tick()
    hat, scale1 = norm_stats(x)
    smalls[0:1] = jnp.sum(d_normed * hat, 0, keepdims=True)
    smalls[1:2] = jnp.sum(d_normed, 0, keepdims=True)
    smalls[4:5] = jnp.sum(d_resid, 0, keepdims=True)
    smalls[5:6] = jnp.sum(d_normed2 * hat2, 0, keepdims=True)
    smalls[6:7] = jnp.sum(d_normed2, 0, keepdims=True)
    smalls[7:8] = jnp.zeros((1, width), F32)
    smalls[8:16] = dot(d_logits, normed2, 1, 0)
    count = width // LANES
    everything = jnp.concatenate([smalls[:, LANES * i : LANES * (i + 1)] for i in range(count)], 0)
    to_near = chunks[6][0]
    share = to_near.shape[1]
    everything = jnp.concatenate([everything, jnp.zeros((n_ex * share - everything.shape[0], LANES), F32)], 0)
    for i in range(n_ex):
        to_near[i] = everything[share * i : share * (i + 1)]
    begin(6)
    tick()
    at["gx_out"][0] = d_resid + norm_back(d_normed, hat, scale1, as_row(at["g1"]))
    tick()
    at["act_out"][0] = resid + dot(comb, slot_out, 0, 0)
    tick()
    for c in PLAN["drain"]:
        advance(c)
    while flying:
        for c in sorted(flying):
            advance(c)


FINISH = ("own", "inner", "small", "act", "gx", "gwout", "gv", "gqk0", "gqk1", "gqk2", "gqk3")


def finish_kernel(*refs):
    n = len(FINISH)
    sources, results, (gin, gdown, gqk_ref, *boxes, loads, stores) = refs[:n], refs[n : n + 15], refs[n + 15 :]
    (act_out, gx_out, g1_ref, b1_ref, gwqkv_out, gbqv_ref, gwout_out, gbout_ref, g2_ref, b2_ref, gkeys_ref,
     gwin_out, gbin_ref, gwdown_out, gbdown_ref) = results
    at = dict(zip(FINISH, boxes))
    coming = dict(zip(FINISH, load(sources, boxes, loads)))
    own_ref, inner_ref, small_ref = at["own"], at["inner"], at["small"]
    width = at["gv"].shape[1]
    owned = own_ref.shape[0]
    blocks, wide = width // LANES, gin.shape[2] // LANES
    pair = 2 * HEAD_DIM
    going = []

    def keep(src, dst):
        copy = pltpu.make_async_copy(src, dst, stores.at[len(going)])
        copy.start()
        going.append(copy)

    for name in ("own", "inner"):
        coming[name].wait()
    for e in range(owned):
        slot_cols = rows_to_columns(own_ref[e])
        hidden_cols = rows_to_columns(inner_ref[e])
        for i in range(blocks):
            col = jnp.broadcast_to(slot_cols[:, i : i + 1], (LANES, LANES))
            for j in range(wide):
                gin[e, LANES * i : LANES * (i + 1), LANES * j : LANES * (j + 1)] = col * inner_ref[e, wide + j : wide + j + 1]
            keep(gin.at[e, pl.ds(LANES * i, LANES)], gwin_out.at[e, pl.ds(LANES * i, LANES)])
        third = wide // 3
        for j in range(wide):
            col = jnp.broadcast_to(hidden_cols[:, j : j + 1], (LANES, LANES))
            for i in range(blocks):
                gdown[e, LANES * j : LANES * (j + 1), LANES * i : LANES * (i + 1)] = col * own_ref[e, 3 + i : 4 + i]
            if (j + 1) % third == 0:
                rows = pl.ds(LANES * (j + 1 - third), LANES * third)
                keep(gdown.at[e, rows], gwdown_out.at[e, rows])
        for j in range(wide):
            gbin_ref[e : e + 1, LANES * j : LANES * (j + 1)] = inner_ref[e, wide + j : wide + j + 1]
        for i in range(blocks):
            gbdown_ref[e : e + 1, LANES * i : LANES * (i + 1)] = own_ref[e, 3 + i : 4 + i]
    for name, out in (("act", act_out), ("gx", gx_out), ("gwout", gwout_out), ("gv", gwqkv_out.at[:, pl.ds(2 * width, width)])):
        coming[name].wait()
        keep(at[name], out)
    for p in range(2):
        coming[f"gqk{p}"].wait()
        for t in range(2):
            keep(at[f"gqk{p}"].at[:, pl.ds(pair * t, pair)], gwqkv_out.at[:, pl.ds(t * width + pair * p, pair)])
    for name in ("gqk2", "gqk3", "small"):
        coming[name].wait()
    one, two = at["gqk2"][...], at["gqk3"][...]
    gqk_ref[0] = jnp.concatenate([one[:, :HEAD_DIM], two[:, :HEAD_DIM]], 1)
    gqk_ref[1] = jnp.concatenate([one[:, HEAD_DIM:], two[:, HEAD_DIM:]], 1)
    for t in range(2):
        keep(gqk_ref.at[t], gwqkv_out.at[:, pl.ds(t * width + 2 * pair, pair)])
    flat = small_ref[...].reshape(-1, LANES)
    rows = jnp.concatenate([flat[16 * i : 16 * (i + 1)] for i in range(blocks)], 1)
    for ref, i in ((g1_ref, 0), (b1_ref, 1), (gbout_ref, 4), (g2_ref, 5), (b2_ref, 6)):
        ref[...] = rows[i : i + 1].reshape(width)
    gbqv_ref[...] = rows[2:4]
    gkeys_ref[...] = rows[8:16]
    for copy in going:
        copy.wait()


def sds(*shape):
    return jax.ShapeDtypeStruct(shape, F32)


def vm(*shape):
    return pltpu.VMEM(shape, F32)


def bv(*shape):
    return pltpu.VMEM(shape, BF)


def dma(*shape):
    return pltpu.SemaphoreType.DMA(shape)


def solution(mesh):
    n_dp, n_ex = mesh.shape["dp"], mesh.shape["expert"]

    def on_device(patches, image_ids, pad_mask, ln1_gain, ln1_bias, w_qkv, bias_qv, w_out, bias_out, ln2_gain, ln2_bias,
                  slot_keys, w_in, bias_in, w_down, bias_down, cotangent):
        _, length, width = patches.shape
        owned, _, hidden = w_in.shape
        experts = owned * n_ex
        wide = hidden // LANES
        share = 16
        pair = 2 * HEAD_DIM
        rounds = powers(n_dp) + powers(n_ex) + HALVINGS
        args = dict(zip(INPUTS, (patches, ln1_gain, ln1_bias, w_qkv, bias_qv, image_ids, w_out, bias_out, ln2_gain, ln2_bias,
                                 slot_keys.T, pad_mask, cotangent, w_in, bias_in, w_down, bias_down)))
        names = [n + "_in" for n in INPUTS]
        outs = {"act_out": sds(1, length, width), "gx_out": sds(1, length, width)}
        scratch = {n: pltpu.VMEM(a.shape, a.dtype) for n, a in args.items()}
        scratch.update(
            joined=vm(3 * width, length), context=vm(width, length), attn=vm(HEADS, length, length), block=vm(length, length),
            high=bv(HEADS, length, length), low=bv(HEADS, length, length), kk=bv(HEADS, pair, length),
            qq=bv(HEADS, pair, length), vt=bv(HEADS, pair, length),
            djoined=vm(3 * width, length), normed=vm(width + 8, length), smalls=vm(16, width),
            stats=vm(experts, 8, LANES), near=vm(n_ex - 1, owned, 8, LANES), mine=vm(owned, 8, LANES),
            far=vm(n_dp, owned, 8, LANES), got=vm(owned, 8, LANES), shared=vm(experts, 8, LANES),
            loads=dma(len(args)), sems=dma(2, 6, max(n_dp, n_ex)))
        widths = (width, width, 2 * pair, 2 * pair, pair, pair)
        for c, (kind, cols) in enumerate(zip(PLAN["kinds"], widths)):
            outs[f"c{c}_1"] = sds(width, cols)
            if kind == "halving":
                pieces = [vm(width >> (i + 1), cols) for i in range(HALVINGS)]
                pieces += [vm(rounds - 2 * HALVINGS, width >> HALVINGS, cols), dma(rounds), dma(rounds)]
            else:
                pieces = [vm(width // 2, cols), vm(3, width // 8, cols), vm(n_dp // 2, width // 8, cols), dma(2, 10 + n_dp // 2)]
            scratch[f"c{c}_0"] = vm(width, cols)
            scratch.update({f"c{c}_{2 + i}": piece for i, piece in enumerate(pieces)})
        scratch.update(c6_0=vm(n_ex, share, LANES), c6_1=vm(n_ex - 1, share, LANES), c6_2=vm(n_dp, share, LANES),
                       c6_3=vm(2, share, LANES))
        outs.update(c6_4=sds(n_ex, share, LANES), own=sds(owned, 8, LANES), inner=sds(owned, 2 * wide, LANES))
        names += list(outs) + list(scratch)
        results = pl.pallas_call(
            functools.partial(layer_kernel, n_dp, n_ex, tuple(names)),
            out_shape=list(outs.values()),
            in_specs=[ANY] * len(args),
            out_specs=[VMEM] * len(outs),
            scratch_shapes=list(scratch.values()),
            compiler_params=pltpu.CompilerParams(collective_id=0, has_side_effects=True, vmem_limit_bytes=LAYER_VMEM),
            name="layer",
        )(*args.values())
        act, gx, *grads, small, own, inner = results
        operands = (own, inner, small, act, gx, *grads)
        act, gx, g1, b1, gwqkv, gbqv, gwout, gbout, g2, b2, gkeys, gwin, gbin, gwdown, gbdown = pl.pallas_call(
            finish_kernel,
            out_shape=(sds(1, length, width), sds(1, length, width), sds(width), sds(width), sds(*w_qkv.shape),
                       sds(*bias_qv.shape), sds(*w_out.shape), sds(width), sds(width), sds(width), sds(experts, width),
                       sds(*w_in.shape), sds(*bias_in.shape), sds(*w_down.shape), sds(*bias_down.shape)),
            in_specs=[ANY] * len(operands),
            out_specs=[ANY, ANY, VMEM, VMEM, ANY, VMEM, ANY, VMEM, VMEM, VMEM, VMEM, ANY, VMEM, ANY, VMEM],
            scratch_shapes=[vm(*w_in.shape), vm(*w_down.shape), vm(2, width, pair), *(vm(*a.shape) for a in operands),
                            dma(len(operands)), dma(10 + 6 * owned)],
            compiler_params=pltpu.CompilerParams(vmem_limit_bytes=FINISH_VMEM),
            name="finish",
        )(*operands)
        return (act, gx, g1, b1, gwqkv, gbqv, gwout, gbout, g2, b2, gkeys.T, gwin, gbin, gwdown, gbdown)

    rows = P(("dp", "expert"), None, None)
    flags = P(("dp", "expert"), None)
    e3, e2 = P("expert", None, None), P("expert", None)
    return jax.shard_map(
        on_device,
        mesh=mesh,
        in_specs=(rows, flags, flags) + (P(),) * 9 + (e3, e2, e3, e2, rows),
        out_specs=(rows, rows) + (P(),) * 9 + (e3, e2, e3, e2),
        check_vma=False,
    )
```

```python
import functools
import math

import jax
import jax.numpy as jnp
from jax import lax
from jax.experimental import pallas as pl
from jax.experimental.pallas import tpu as pltpu
from jax.sharding import PartitionSpec as P

HEADS = 6
HEAD_DIM = 64
LANES = 128
EPSILON = 1e-06
NEGATIVE = -1e30
HIGH = lax.Precision.HIGH
BF = jnp.bfloat16
F32 = jnp.float32
MESH = pl.DeviceIdType.MESH
LAYER_VMEM = 56 << 20
FINISH_VMEM = 56 << 20
PLAN = {
    "kinds": ('direct', 'direct', 'direct', 'direct', 'direct', 'direct', 'small'),
    "ticks": {3: (0,), 10: (1,), 12: (0,), 13: (2,), 17: (3,), 18: (1,), 19: (4, 2), 20: (5,)},
    "drain": (0, 3, 6, 4, 5, 1, 0, 0, 2, 1, 3, 1, 6, 2, 4, 2, 5, 6, 3, 3, 4, 4, 5, 5),
}
VMEM = pl.BlockSpec(memory_space=pltpu.VMEM)
ANY = pl.BlockSpec(memory_space=pl.ANY)


def dot(left, right, dim_left, dim_right, precision=HIGH):
    return lax.dot_general(
        left, right, (((dim_left,), (dim_right,)), ((), ())), precision=precision, preferred_element_type=F32
    )


def parts(value):
    high = value.astype(BF)
    return high, (value - high.astype(F32)).astype(BF)


def norm_stats(values):
    center = values - jnp.mean(values, -1, keepdims=True)
    spread = jnp.mean(center * center, -1, keepdims=True)
    scale = lax.rsqrt(spread + EPSILON)
    return center * scale, scale


def load(sources, targets, sems):
    copies = [pltpu.make_async_copy(src, dst, sems.at[i]) for i, (src, dst) in enumerate(zip(sources, targets))]
    for copy in copies:
        copy.start()
    return copies


def greet(n_dp, n_ex, dp, ex):
    barrier = pltpu.get_barrier_semaphore()
    for i in range(1, n_ex):
        pl.semaphore_signal(barrier, inc=1, device_id=(dp, lax.rem(ex + i, n_ex)), device_id_type=MESH)
    for i in range(1, n_dp):
        pl.semaphore_signal(barrier, inc=1, device_id=(lax.rem(dp + i, n_dp), ex), device_id_type=MESH)
    return lambda: pl.semaphore_wait(barrier, n_ex + n_dp - 2)


def send(src, dst, out_sem, in_sem, dp, ex):
    copy = pltpu.make_async_remote_copy(
        src_ref=src, dst_ref=dst, send_sem=out_sem, recv_sem=in_sem, device_id=(dp, ex), device_id_type=MESH)
    copy.start()
    return copy


def as_row(ref):
    return ref[...].reshape(1, -1)


def to_tiles(rows):
    return jnp.stack([jnp.concatenate([rows[e : e + 1, LANES * i : LANES * (i + 1)] for i in range(8)], 0) for e in range(rows.shape[0])], 0)


def from_tiles(tiles, first, count):
    return jnp.concatenate([tiles[:, first + i, :] for i in range(count)], -1)


def merge(tiles):
    peaks = [tile[:, 6:7, :] for tile in tiles]
    peak = functools.reduce(jnp.maximum, peaks)
    row = lax.broadcasted_iota(jnp.int32, tiles[0].shape, 1)
    weighted = (row < 3) | (row == 7)
    total = None
    for tile, own in zip(tiles, peaks):
        scaled = jnp.where(weighted, tile * jnp.exp(own - peak), tile)
        total = scaled if total is None else total + scaled
    return jnp.where(row == 6, peak, total)


def gelu_parts(inner):
    phi = 0.5 * (1.0 + lax.erf(inner * (1.0 / math.sqrt(2.0))))
    density = jnp.exp(-0.5 * inner * inner) * (1.0 / math.sqrt(2.0 * math.pi))
    return inner * phi, phi + inner * density


def rows_to_columns(rows):
    pad = -rows.shape[0] % 8
    if pad:
        rows = jnp.concatenate([rows, jnp.zeros((pad, LANES), F32)], 0)
    return rows.T


def times_columns(cols, count, w_ref, e, lanes):
    wide = [jnp.broadcast_to(cols[:, i : i + 1], (LANES, LANES)) for i in range(count)]
    rows = []
    for j in range(lanes):
        acc = None
        for i in range(count):
            term = wide[i] * w_ref[e, LANES * i : LANES * (i + 1), LANES * j : LANES * (j + 1)]
            term = jnp.sum(term.reshape(LANES // 8, 8, LANES), 0)
            acc = term if acc is None else acc + term
        rows.append(jnp.sum(acc, 0, keepdims=True))
    return jnp.concatenate(rows, 0)


def times_rows(rows, count, w_ref, e, blocks):
    out = []
    for i in range(blocks):
        acc = None
        for j in range(count):
            term = rows[j : j + 1] * w_ref[e, LANES * i : LANES * (i + 1), LANES * j : LANES * (j + 1)]
            acc = term if acc is None else acc + term
        out.append(jnp.sum(acc.T, 0, keepdims=True))
    return jnp.concatenate(out, 0)


def norm_back(grad, hat, scale, gain):
    g = grad * gain
    return scale * (g - jnp.mean(g, -1, keepdims=True) - hat * jnp.mean(g * hat, -1, keepdims=True))


def powers(n):
    return n.bit_length() - 1


HALVINGS = 4
INPUTS = ("x", "g1", "b1", "wqkv", "bqv", "ids", "wout", "bout", "g2", "b2", "keys", "live", "cot", "win", "bin", "wdown", "bdown")


def layer_kernel(n_dp, n_ex, names, *refs):
    at = dict(zip(names, refs))
    dp, ex = lax.axis_index("dp"), lax.axis_index("expert")
    stats_ref, near, mine, far, got, shared_ref, own_ref, inner_ref = (
        at[n] for n in ("stats", "near", "mine", "far", "got", "shared", "own", "inner"))
    win, wdown, bin_ref, bdown_ref = at["win"], at["wdown"], at["bin"], at["bdown"]
    joined_ref, context_ref, attn_ref, share_ref = at["joined"], at["context"], at["attn"], at["share"]
    high_ref, low_ref, kk_ref, qq_ref, vt_ref = at["high"], at["low"], at["kk"], at["qq"], at["vt"]
    djoined_ref, normed_ref, smalls = at["djoined"], at["normed"], at["smalls"]
    sems = at["sems"]
    owned = win.shape[0]
    all_here = greet(n_dp, n_ex, dp, ex)
    coming = dict(zip(INPUTS, load([at[n + "_in"] for n in INPUTS], [at[n] for n in INPUTS], at["loads"])))

    def ready(*which):
        for n in which:
            coming[n].wait()

    ready("x", "g1", "b1")
    x = at["x"][0]
    length, width = x.shape
    pair = 2 * HEAD_DIM
    half = length // 2
    halves = [slice(half * b, half * (b + 1)) for b in range(2)]
    hat, _ = norm_stats(x)
    normed = hat * as_row(at["g1"]) + as_row(at["b1"])
    ready("wqkv", "bqv", "ids")
    joined = dot(at["wqkv"][...], normed, 0, 1)
    bias = jnp.broadcast_to(at["bqv"][0:1], (8, width)).T[:, :1]
    bias_v = jnp.broadcast_to(at["bqv"][1:2], (8, width)).T[:, :1]
    scale = 1.0 / math.sqrt(HEAD_DIM)
    joined_ref[0:width] = (joined[:width] + bias) * scale
    joined_ref[width : 2 * width] = joined[width : 2 * width]
    joined_ref[2 * width :] = joined[2 * width :] + bias_v
    place = lax.broadcasted_iota(jnp.int32, (16, length), 0)
    same = place == at["ids"][...]
    pick = jnp.where(same, 1.0, 0.0).astype(BF)
    bar = jnp.where(same, 0.0, NEGATIVE).astype(BF)
    ones = jnp.ones((16, length), BF)
    for h in range(HEADS):
        lo = HEAD_DIM * h
        q_hi, q_lo = parts(joined_ref[lo : lo + HEAD_DIM])
        k_hi, k_lo = parts(joined_ref[width + lo : width + lo + HEAD_DIM])
        v_hi, v_lo = parts(joined_ref[2 * width + lo : 2 * width + lo + HEAD_DIM])
        queries = jnp.concatenate([q_hi, q_hi, q_lo, pick], 0)
        keys = jnp.concatenate([k_hi, k_lo, k_hi, bar], 0).T
        values = jnp.concatenate([v_hi, v_lo, ones], 0)
        values_low = jnp.concatenate([v_hi, ones], 0)
        kk_ref[h] = jnp.concatenate([k_hi, k_lo], 0)
        qq_ref[h] = jnp.concatenate([q_hi, q_lo], 0)
        vt_ref[h] = values[:pair]
        for part in halves:
            scores = dot(keys, queries[:, part], 1, 0, None)
            expo = jnp.exp(scores - jnp.max(scores, 0, keepdims=True))
            attn_ref[h, :, part] = expo
            p_hi, p_lo = parts(expo)
            high_ref[h, :, part] = p_hi
            low_ref[h, :, part] = p_lo
            both = dot(values, p_hi, 1, 0, None)
            rest = dot(values_low, p_lo, 1, 0, None)
            share = 1.0 / (both[pair : pair + 1] + rest[HEAD_DIM : HEAD_DIM + 1])
            share_ref[h : h + 1, part] = share
            context_ref[lo : lo + HEAD_DIM, part] = (both[:HEAD_DIM] + both[HEAD_DIM:pair] + rest[:HEAD_DIM]) * share
    ready("wout", "bout", "g2", "b2", "keys", "live", "cot")
    context = context_ref[...]
    resid = x + dot(context, at["wout"][...], 0, 0) + as_row(at["bout"])
    gain2 = as_row(at["g2"])
    hat2, scale2 = norm_stats(resid)
    normed2 = hat2 * gain2 + as_row(at["b2"])
    logits = dot(at["keys"][...], normed2, 1, 1)
    masked = jnp.where(at["live"][...] > 0, logits, NEGATIVE)
    peak = jnp.max(masked, 1, keepdims=True)
    expo = jnp.exp(masked - peak)
    total = jnp.sum(expo, 1, keepdims=True)
    summed = dot(expo, normed2, 1, 0)
    comb = jnp.exp(logits - jnp.max(logits, 0, keepdims=True))
    comb = comb * (1.0 / jnp.sum(comb, 0, keepdims=True))
    cot = at["cot"][0]
    part_out = dot(comb, cot, 1, 0)
    experts = logits.shape[0]
    stats_ref[...] = to_tiles(jnp.concatenate(
        [summed, part_out, jnp.broadcast_to(peak, (experts, LANES)), jnp.broadcast_to(total, (experts, LANES))], 1))
    all_here()
    copies = []
    for i in range(1, n_ex):
        to = lax.rem(ex + i, n_ex)
        copies.append(send(stats_ref.at[pl.ds(to * owned, owned)], near.at[i - 1], sems.at[0, 0, i], sems.at[1, 0, i], dp, to))
    normed_ref[0:width] = normed.T
    normed_ref[width:] = jnp.ones((8, length), F32)
    for copy in copies:
        copy.wait()
    mine[...] = merge([stats_ref[pl.ds(ex * owned, owned)]] + [near[i] for i in range(n_ex - 1)])
    copies = []
    for i in range(1, n_dp):
        copies.append(send(mine, far.at[dp], sems.at[0, 1, i], sems.at[1, 1, i], lax.rem(dp + i, n_dp), ex))
    far[dp] = mine[...]
    ready("win", "bin", "wdown", "bdown")
    for copy in copies:
        copy.wait()
    tiles = merge([far[i] for i in range(n_dp)])
    blocks, wide = win.shape[1] // LANES, win.shape[2] // LANES
    for e in range(owned):
        tile = tiles[e]
        slots = tile[0:blocks] / tile[7:8]
        d_out = tile[3 : 3 + blocks]
        bias = jnp.concatenate([bin_ref[e : e + 1, LANES * j : LANES * (j + 1)] for j in range(wide)], 0)
        inner = times_columns(rows_to_columns(slots), blocks, win, e, wide) + bias
        hidden, slope = gelu_parts(inner)
        bias = jnp.concatenate([bdown_ref[e : e + 1, LANES * j : LANES * (j + 1)] for j in range(blocks)], 0)
        out = times_columns(rows_to_columns(hidden), wide, wdown, e, blocks) + bias
        d_inner = times_rows(d_out, blocks, wdown, e, wide) * slope
        d_slots = times_rows(d_inner, wide, win, e, blocks)
        along = jnp.sum(slots * d_slots, keepdims=True)
        lane = lax.broadcasted_iota(jnp.int32, (1, LANES), 1)
        last = jnp.where(lane < LANES // 2, tile[7:8], along)
        result = jnp.concatenate([out, d_slots, tile[6:7], last], 0)
        got[e] = result
        shared_ref[ex * owned + e] = result
        own_ref[e] = jnp.concatenate([slots, d_out, jnp.zeros((2, LANES), F32)], 0)
        inner_ref[e] = jnp.concatenate([hidden, d_inner], 0)
    copies = []
    for i in range(1, n_ex):
        copies.append(send(got, shared_ref.at[pl.ds(ex * owned, owned)], sems.at[0, 2, i], sems.at[1, 2, i], dp, lax.rem(ex + i, n_ex)))
    for copy in copies:
        copy.wait()

    bits = [("expert", 0)] + [("expert", b) for b in range(1, powers(n_ex))] + [("dp", b) for b in range(powers(n_dp))]

    def bit_of(which):
        axis, b = which
        return lax.rem((ex if axis == "expert" else dp) // (1 << b), 2)

    def flip(which, weight=1):
        axis, b = which
        step = (1 - 2 * bit_of(which)) * (1 << b) * weight
        return (0, step) if axis == "expert" else (step, 0)

    first = bit_of(bits[0])
    steps = []
    for i, which in enumerate(bits):
        if i in (1, 2):
            other = bits[3 - i]
            one, two = flip(which, 1 - first), flip(other, first)
            bit = bit_of(which) * (1 - first) + bit_of(other) * first
            steps.append((bit, (one[0] + two[0], one[1] + two[1])))
        else:
            steps.append((bit_of(which), flip(which)))
    exchanges = len(bits)

    def halving(chunk):
        part, total, *boxes, send_sem, recv_sem = chunk
        rows = part.shape[0]
        offsets = [0]
        for i in range(HALVINGS):
            offsets.append(pl.multiple_of(offsets[-1] + steps[i][0] * (rows >> (i + 1)), 8))
        final = pl.ds(offsets[HALVINGS], rows >> HALVINGS)

        def start(i):
            partner = steps[i if i < exchanges else exchanges + HALVINGS - 1 - i][1]
            if i < HALVINGS:
                size = rows >> (i + 1)
                away = pl.multiple_of(offsets[i] + (1 - steps[i][0]) * size, 8)
                src, dst = part.at[pl.ds(away, size)], boxes[i]
            elif i < exchanges:
                src, dst = part.at[final], boxes[HALVINGS].at[i - HALVINGS]
            else:
                level = exchanges + HALVINGS - i
                src = dst = total.at[pl.ds(offsets[level], rows >> level)]
            return [send(src, dst, send_sem.at[i], recv_sem.at[i], dp + partner[0], ex + partner[1])]

        def absorb(i):
            if i < HALVINGS:
                where = pl.ds(offsets[i + 1], rows >> (i + 1))
                part[where] = part[where] + boxes[i][...]
            elif i < exchanges - 1:
                part[final] = part[final] + boxes[HALVINGS][i - HALVINGS]
            elif i == exchanges - 1:
                total[final] = part[final] + boxes[HALVINGS][i - HALVINGS]

        return start, absorb, exchanges + HALVINGS

    x_bit, y_bit = bit_of(("expert", 1)), bit_of(("dp", 0))
    deep, n_deep = dp // 2, n_dp // 2

    def direct(chunk):
        part, total, box_core, box_plane, box_deep, wires = chunk
        rows = part.shape[0]
        half, quarter = rows // 2, rows // 8
        base = pl.multiple_of(first * half, 8)
        away = pl.multiple_of((1 - first) * half, 8)

        def spot(j):
            flip_x, flip_y = j % 2, j // 2
            to_x = x_bit + (1 - 2 * x_bit) * flip_x
            to_y = y_bit + (1 - 2 * y_bit) * flip_y
            row = pl.multiple_of(base + quarter * (to_x + 2 * to_y), 8)
            return pl.ds(row, quarter), dp + (to_y - y_bit), ex + 2 * (to_x - x_bit)

        own = spot(0)[0]

        def start(i):
            if i in (0, 4):
                core = (dp, ex + 1 - 2 * first)
                src, dst = (part.at[pl.ds(away, half)], box_core) if i == 0 else (total.at[pl.ds(base, half)],) * 2
                return [send(src, dst, wires.at[0, i], wires.at[1, i], *core)]
            copies = []
            if i == 2:
                for k in range(1, n_deep):
                    copies.append(send(part.at[own], box_deep.at[deep], wires.at[0, 10 + k], wires.at[1, 10 + k], lax.rem(dp + 2 * k, n_dp), ex))
                box_deep[deep] = part[own]
            else:
                for j in range(1, 4):
                    where, to_dp, to_ex = spot(j)
                    src, dst = (part.at[where], box_plane.at[j - 1]) if i == 1 else (total.at[own],) * 2
                    at = (4 if i == 1 else 7) + j
                    copies.append(send(src, dst, wires.at[0, at], wires.at[1, at], to_dp, to_ex))
            return copies

        def absorb(i):
            if i == 0:
                part[pl.ds(base, half)] = part[pl.ds(base, half)] + box_core[...]
            elif i == 1:
                part[own] = (part[own] + box_plane[0]) + (box_plane[1] + box_plane[2])
            elif i == 2:
                total[own] = functools.reduce(jnp.add, [box_deep[k] for k in range(n_deep)])

        return start, absorb, 5

    def small(chunk):
        to_near, from_near, from_far, local, result = chunk

        def start(i):
            copies = []
            if i == 1:
                for k in range(1, n_dp):
                    copies.append(send(local.at[0], from_far.at[dp], sems.at[0, 4, k], sems.at[1, 4, k], lax.rem(dp + k, n_dp), ex))
                from_far[dp] = local[0]
                return copies
            for k in range(1, n_ex):
                to = lax.rem(ex + k, n_ex)
                src, dst = (to_near.at[to], from_near.at[k - 1]) if i == 0 else (local.at[1], result.at[ex])
                copies.append(send(src, dst, sems.at[0, 3 + i, k], sems.at[1, 3 + i, k], dp, to))
            if i == 2:
                result[ex] = local[1]
            return copies

        def absorb(i):
            if i == 0:
                local[0] = functools.reduce(jnp.add, [to_near[ex]] + [from_near[k] for k in range(n_ex - 1)])
            elif i == 1:
                local[1] = functools.reduce(jnp.add, [from_far[k] for k in range(n_dp)])

        return start, absorb, 3

    kinds = {"halving": halving, "direct": direct, "small": small}
    chunks = [[at[f"c{c}_{i}"] for i in range(sum(n.startswith(f"c{c}_") for n in names))] for c in range(len(PLAN["kinds"]))]
    flying = {}
    slot = [0]

    def begin(c):
        start, absorb, rounds = kinds[PLAN["kinds"][c]](chunks[c])
        flying[c] = [start, absorb, rounds, 0, start(0)]

    def advance(c):
        if c not in flying:
            return
        start, absorb, rounds, i, copies = flying[c]
        for copy in copies:
            copy.wait()
        absorb(i)
        if i + 1 < rounds:
            flying[c][3:] = [i + 1, start(i + 1)]
        else:
            del flying[c]

    def tick():
        for c in PLAN["ticks"].get(slot[0], ()):
            advance(c)
        slot[0] += 1

    shared = shared_ref[...]
    slot_out = from_tiles(shared, 0, 3)
    d_slots = from_tiles(shared, 3, 3)
    peak = shared[:, 6, 0:1]
    total = shared[:, 7, 0:1]
    along = shared[:, 7, LANES - 1 : LANES]
    dispatch = jnp.exp(masked - peak) / total
    d_comb = dot(slot_out, cot, 1, 1)
    d_logits = comb * (d_comb - jnp.sum(comb * d_comb, 0, keepdims=True))
    d_logits = d_logits + dispatch * (dot(d_slots, normed2, 1, 1) - along)
    d_normed2 = dot(jnp.concatenate([dispatch, d_logits], 0), jnp.concatenate([d_slots, at["keys"][...]], 0), 0, 0)
    d_resid = cot + norm_back(d_normed2, hat2, scale2, gain2)
    chunks[0][0][...] = dot(context_ref[...], d_resid, 1, 0)
    begin(0)
    d_context = dot(at["wout"][...], d_resid, 1, 1)
    tick()
    outs = []
    for h in range(HEADS):
        lo = HEAD_DIM * h
        scaled = d_context[lo : lo + HEAD_DIM] * share_ref[h : h + 1]
        o_hi, o_lo = parts(scaled)
        rowsum = jnp.sum(scaled * context_ref[lo : lo + HEAD_DIM], 0, keepdims=True)
        r_hi = rowsum.astype(BF).astype(F32)
        r_mid = (rowsum - r_hi).astype(BF).astype(F32)
        r_all = jnp.where(place == 0, r_hi, jnp.where(place == 1, r_mid, jnp.where(place == 2, rowsum - r_hi - r_mid, 0.0)))
        outs.append(jnp.concatenate([o_hi, o_hi, o_lo, r_all.astype(BF)], 0))
        both = jnp.concatenate([o_hi, o_lo], 0)
        d_v = None
        for part in halves:
            high = dot(both[:, part], high_ref[h, :, part], 1, 1, None)
            term = high[:HEAD_DIM] + high[HEAD_DIM:] + dot(o_hi[:, part], low_ref[h, :, part], 1, 1, None)
            d_v = term if d_v is None else d_v + term
        djoined_ref[2 * width + lo : 2 * width + lo + HEAD_DIM] = d_v
        tick()
    grad = dot(normed_ref[...], djoined_ref[2 * width :], 1, 1)
    chunks[1][0][...] = grad[:width]
    begin(1)
    smalls[3:4] = grad[width : width + 1]
    minus = jnp.where(place < 3, -1.0, 0.0).astype(BF)
    launch_at = {1: (2, 0, 2), 3: (3, 2, 4), 4: (4, 4, 5), 5: (5, 5, 6)}
    for h in range(HEADS):
        lo = HEAD_DIM * h
        span = slice(lo, lo + HEAD_DIM)
        d_out = outs[h]
        v_both, keys, queries = vt_ref[h], kk_ref[h], qq_ref[h]
        values = jnp.concatenate([v_both, v_both[:HEAD_DIM], minus], 0).T
        d_k = None
        for part in halves:
            s_hi, s_lo = parts(attn_ref[h, :, part] * dot(values, d_out[:, part], 1, 0, None))
            both = dot(keys, s_hi, 1, 0, None)
            d_q = both[:HEAD_DIM] + both[HEAD_DIM:] + dot(keys[:HEAD_DIM], s_lo, 1, 0, None)
            djoined_ref[span, part] = d_q * scale
            both = dot(queries[:, part], s_hi, 1, 1, None)
            term = both[:HEAD_DIM] + both[HEAD_DIM:] + dot(queries[:HEAD_DIM, part], s_lo, 1, 1, None)
            d_k = term if d_k is None else d_k + term
            tick()
        djoined_ref[width + lo : width + lo + HEAD_DIM] = d_k
        if h in launch_at:
            c, lo, hi = launch_at[h]
            lo, hi = lo * HEAD_DIM, hi * HEAD_DIM
            d_part = jnp.concatenate([djoined_ref[lo:hi], djoined_ref[width + lo : width + hi]], 0)
            grad = dot(normed_ref[...], d_part, 1, 1)
            chunks[c][0][...] = grad[:width]
            begin(c)
            row = grad[width : width + 1, : hi - lo]
            if (hi - lo) % LANES == 0:
                smalls[2:3, lo:hi] = row
            elif lo % LANES == 0:
                kept_row = row
            else:
                smalls[2:3, lo - HEAD_DIM : hi] = jnp.concatenate([kept_row, row], 1)
    d_normed = dot(djoined_ref[...], at["wqkv"][...], 0, 1)
    tick()
    hat, scale1 = norm_stats(x)
    smalls[0:1] = jnp.sum(d_normed * hat, 0, keepdims=True)
    smalls[1:2] = jnp.sum(d_normed, 0, keepdims=True)
    smalls[4:5] = jnp.sum(d_resid, 0, keepdims=True)
    smalls[5:6] = jnp.sum(d_normed2 * hat2, 0, keepdims=True)
    smalls[6:7] = jnp.sum(d_normed2, 0, keepdims=True)
    smalls[7:8] = jnp.zeros((1, width), F32)
    smalls[8:16] = dot(d_logits, normed2, 1, 0)
    count = width // LANES
    everything = jnp.concatenate([smalls[:, LANES * i : LANES * (i + 1)] for i in range(count)], 0)
    to_near = chunks[6][0]
    share = to_near.shape[1]
    everything = jnp.concatenate([everything, jnp.zeros((n_ex * share - everything.shape[0], LANES), F32)], 0)
    for i in range(n_ex):
        to_near[i] = everything[share * i : share * (i + 1)]
    begin(6)
    tick()
    at["gx_out"][0] = d_resid + norm_back(d_normed, hat, scale1, as_row(at["g1"]))
    tick()
    at["act_out"][0] = resid + dot(comb, slot_out, 0, 0)
    tick()
    for c in PLAN["drain"]:
        advance(c)
    while flying:
        for c in sorted(flying):
            advance(c)


FINISH = ("own", "inner", "small", "act", "gx", "gwout", "gv", "gqk0", "gqk1", "gqk2", "gqk3")


def finish_kernel(*refs):
    n = len(FINISH)
    sources, results, (gin, gdown, gqk_ref, *boxes, loads, stores) = refs[:n], refs[n : n + 15], refs[n + 15 :]
    (act_out, gx_out, g1_ref, b1_ref, gwqkv_out, gbqv_ref, gwout_out, gbout_ref, g2_ref, b2_ref, gkeys_ref,
     gwin_out, gbin_ref, gwdown_out, gbdown_ref) = results
    at = dict(zip(FINISH, boxes))
    coming = dict(zip(FINISH, load(sources, boxes, loads)))
    own_ref, inner_ref, small_ref = at["own"], at["inner"], at["small"]
    width = at["gv"].shape[1]
    owned = own_ref.shape[0]
    blocks, wide = width // LANES, gin.shape[2] // LANES
    pair = 2 * HEAD_DIM
    going = []

    def keep(src, dst):
        copy = pltpu.make_async_copy(src, dst, stores.at[len(going)])
        copy.start()
        going.append(copy)

    for name in ("own", "inner"):
        coming[name].wait()
    for e in range(owned):
        slot_cols = rows_to_columns(own_ref[e])
        hidden_cols = rows_to_columns(inner_ref[e])
        for i in range(blocks):
            col = jnp.broadcast_to(slot_cols[:, i : i + 1], (LANES, LANES))
            for j in range(wide):
                gin[e, LANES * i : LANES * (i + 1), LANES * j : LANES * (j + 1)] = col * inner_ref[e, wide + j : wide + j + 1]
            keep(gin.at[e, pl.ds(LANES * i, LANES)], gwin_out.at[e, pl.ds(LANES * i, LANES)])
        third = wide // 3
        for j in range(wide):
            col = jnp.broadcast_to(hidden_cols[:, j : j + 1], (LANES, LANES))
            for i in range(blocks):
                gdown[e, LANES * j : LANES * (j + 1), LANES * i : LANES * (i + 1)] = col * own_ref[e, 3 + i : 4 + i]
            if (j + 1) % third == 0:
                rows = pl.ds(LANES * (j + 1 - third), LANES * third)
                keep(gdown.at[e, rows], gwdown_out.at[e, rows])
        for j in range(wide):
            gbin_ref[e : e + 1, LANES * j : LANES * (j + 1)] = inner_ref[e, wide + j : wide + j + 1]
        for i in range(blocks):
            gbdown_ref[e : e + 1, LANES * i : LANES * (i + 1)] = own_ref[e, 3 + i : 4 + i]
    for name, out in (("act", act_out), ("gx", gx_out), ("gwout", gwout_out), ("gv", gwqkv_out.at[:, pl.ds(2 * width, width)])):
        coming[name].wait()
        keep(at[name], out)
    for p in range(2):
        coming[f"gqk{p}"].wait()
        for t in range(2):
            keep(at[f"gqk{p}"].at[:, pl.ds(pair * t, pair)], gwqkv_out.at[:, pl.ds(t * width + pair * p, pair)])
    for name in ("gqk2", "gqk3", "small"):
        coming[name].wait()
    one, two = at["gqk2"][...], at["gqk3"][...]
    gqk_ref[0] = jnp.concatenate([one[:, :HEAD_DIM], two[:, :HEAD_DIM]], 1)
    gqk_ref[1] = jnp.concatenate([one[:, HEAD_DIM:], two[:, HEAD_DIM:]], 1)
    for t in range(2):
        keep(gqk_ref.at[t], gwqkv_out.at[:, pl.ds(t * width + 2 * pair, pair)])
    flat = small_ref[...].reshape(-1, LANES)
    rows = jnp.concatenate([flat[16 * i : 16 * (i + 1)] for i in range(blocks)], 1)
    for ref, i in ((g1_ref, 0), (b1_ref, 1), (gbout_ref, 4), (g2_ref, 5), (b2_ref, 6)):
        ref[...] = rows[i : i + 1].reshape(width)
    gbqv_ref[...] = rows[2:4]
    gkeys_ref[...] = rows[8:16]
    for copy in going:
        copy.wait()


def sds(*shape):
    return jax.ShapeDtypeStruct(shape, F32)


def vm(*shape):
    return pltpu.VMEM(shape, F32)


def bv(*shape):
    return pltpu.VMEM(shape, BF)


def dma(*shape):
    return pltpu.SemaphoreType.DMA(shape)


def solution(mesh):
    n_dp, n_ex = mesh.shape["dp"], mesh.shape["expert"]

    def on_device(patches, image_ids, pad_mask, ln1_gain, ln1_bias, w_qkv, bias_qv, w_out, bias_out, ln2_gain, ln2_bias,
                  slot_keys, w_in, bias_in, w_down, bias_down, cotangent):
        _, length, width = patches.shape
        owned, _, hidden = w_in.shape
        experts = owned * n_ex
        wide = hidden // LANES
        share = 16
        pair = 2 * HEAD_DIM
        rounds = powers(n_dp) + powers(n_ex) + HALVINGS
        args = dict(zip(INPUTS, (patches, ln1_gain, ln1_bias, w_qkv, bias_qv, image_ids, w_out, bias_out, ln2_gain, ln2_bias,
                                 slot_keys.T, pad_mask, cotangent, w_in, bias_in, w_down, bias_down)))
        names = [n + "_in" for n in INPUTS]
        outs = {"act_out": sds(1, length, width), "gx_out": sds(1, length, width)}
        scratch = {n: pltpu.VMEM(a.shape, a.dtype) for n, a in args.items()}
        scratch.update(
            joined=vm(3 * width, length), context=vm(width, length), attn=vm(HEADS, length, length), share=vm(8, length),
            high=bv(HEADS, length, length), low=bv(HEADS, length, length), kk=bv(HEADS, pair, length),
            qq=bv(HEADS, pair, length), vt=bv(HEADS, pair, length),
            djoined=vm(3 * width, length), normed=vm(width + 8, length), smalls=vm(16, width),
            stats=vm(experts, 8, LANES), near=vm(n_ex - 1, owned, 8, LANES), mine=vm(owned, 8, LANES),
            far=vm(n_dp, owned, 8, LANES), got=vm(owned, 8, LANES), shared=vm(experts, 8, LANES),
            loads=dma(len(args)), sems=dma(2, 6, max(n_dp, n_ex)))
        widths = (width, width, 2 * pair, 2 * pair, pair, pair)
        for c, (kind, cols) in enumerate(zip(PLAN["kinds"], widths)):
            outs[f"c{c}_1"] = sds(width, cols)
            if kind == "halving":
                pieces = [vm(width >> (i + 1), cols) for i in range(HALVINGS)]
                pieces += [vm(rounds - 2 * HALVINGS, width >> HALVINGS, cols), dma(rounds), dma(rounds)]
            else:
                pieces = [vm(width // 2, cols), vm(3, width // 8, cols), vm(n_dp // 2, width // 8, cols), dma(2, 10 + n_dp // 2)]
            scratch[f"c{c}_0"] = vm(width, cols)
            scratch.update({f"c{c}_{2 + i}": piece for i, piece in enumerate(pieces)})
        scratch.update(c6_0=vm(n_ex, share, LANES), c6_1=vm(n_ex - 1, share, LANES), c6_2=vm(n_dp, share, LANES),
                       c6_3=vm(2, share, LANES))
        outs.update(c6_4=sds(n_ex, share, LANES), own=sds(owned, 8, LANES), inner=sds(owned, 2 * wide, LANES))
        names += list(outs) + list(scratch)
        results = pl.pallas_call(
            functools.partial(layer_kernel, n_dp, n_ex, tuple(names)),
            out_shape=list(outs.values()),
            in_specs=[ANY] * len(args),
            out_specs=[VMEM] * len(outs),
            scratch_shapes=list(scratch.values()),
            compiler_params=pltpu.CompilerParams(collective_id=0, has_side_effects=True, vmem_limit_bytes=LAYER_VMEM),
            name="layer",
        )(*args.values())
        act, gx, *grads, small, own, inner = results
        operands = (own, inner, small, act, gx, *grads)
        act, gx, g1, b1, gwqkv, gbqv, gwout, gbout, g2, b2, gkeys, gwin, gbin, gwdown, gbdown = pl.pallas_call(
            finish_kernel,
            out_shape=(sds(1, length, width), sds(1, length, width), sds(width), sds(width), sds(*w_qkv.shape),
                       sds(*bias_qv.shape), sds(*w_out.shape), sds(width), sds(width), sds(width), sds(experts, width),
                       sds(*w_in.shape), sds(*bias_in.shape), sds(*w_down.shape), sds(*bias_down.shape)),
            in_specs=[ANY] * len(operands),
            out_specs=[ANY, ANY, VMEM, VMEM, ANY, VMEM, ANY, VMEM, VMEM, VMEM, VMEM, ANY, VMEM, ANY, VMEM],
            scratch_shapes=[vm(*w_in.shape), vm(*w_down.shape), vm(2, width, pair), *(vm(*a.shape) for a in operands),
                            dma(len(operands)), dma(10 + 6 * owned)],
            compiler_params=pltpu.CompilerParams(vmem_limit_bytes=FINISH_VMEM),
            name="finish",
        )(*operands)
        return (act, gx, g1, b1, gwqkv, gbqv, gwout, gbout, g2, b2, gkeys.T, gwin, gbin, gwdown, gbdown)

    rows = P(("dp", "expert"), None, None)
    flags = P(("dp", "expert"), None)
    e3, e2 = P("expert", None, None), P("expert", None)
    return jax.shard_map(
        on_device,
        mesh=mesh,
        in_specs=(rows, flags, flags) + (P(),) * 9 + (e3, e2, e3, e2, rows),
        out_specs=(rows, rows) + (P(),) * 9 + (e3, e2, e3, e2),
        check_vma=False,
    )
```
